32 devices in a mesh: dp: 16 (over z, x, core), ctx: 2 (over y).
Axes of the slice: x: 2, y: 2, z: 4, core: 2. Of those that a mesh axis runs over, the one named last changes fastest.
Arguments:
- tokens_in: bfloat16 [16, 768, 1152], P('dp', 'ctx'), may hold values from -6 to 6
- cotangent: float32 [16, 768, 1152], P('dp', 'ctx'), may hold values from -6 to 6
- token_mask: int32 [16, 768], P('dp', 'ctx'), may hold values from 0 to 1, as said below
- attn_params: float32 [1152, 4613], P(('dp', 'ctx'))
- attn_first: float32 [1152, 4613], P(('dp', 'ctx')), may hold values from -60 to 60
- attn_second: float32 [1152, 4613], P(('dp', 'ctx')), may hold values from 1 to 100
- feed_params: float32 [1152, 8611], P(('dp', 'ctx'))
- feed_first: float32 [1152, 8611], P(('dp', 'ctx')), may hold values from -60 to 60
- feed_second: float32 [1152, 8611], P(('dp', 'ctx')), may hold values from 1 to 100
- up_bias: float32 [4304], replicated, may hold values from -3 to 3
- up_bias_first: float32 [4304], replicated, may hold values from -60 to 60
- up_bias_second: float32 [4304], replicated, may hold values from 1 to 100
Outputs:
- block_out: float32 [16, 768, 1152], P('dp', 'ctx')
- grad_input: float32 [16, 768, 1152], P('dp', 'ctx')
- grad_attn: float32 [1152, 4613], P(('dp', 'ctx'))
- grad_feed: float32 [1152, 8611], P(('dp', 'ctx'))
- grad_up_bias: float32 [4304], replicated
- new_attn: float32 [1152, 4613], P(('dp', 'ctx'))
- new_attn_first: float32 [1152, 4613], P(('dp', 'ctx'))
- new_attn_second: float32 [1152, 4613], P(('dp', 'ctx'))
- new_feed: float32 [1152, 8611], P(('dp', 'ctx'))
- new_feed_first: float32 [1152, 8611], P(('dp', 'ctx'))
- new_feed_second: float32 [1152, 8611], P(('dp', 'ctx'))
- new_up_bias: float32 [4304], replicated
- new_up_bias_first: float32 [4304], replicated
- new_up_bias_second: float32 [4304], replicated
The draws below stay inside these ranges and needn't reach their ends.
Inputs may be any that keep to these rules, and one draw needn't show every extreme that they name: `token_mask`: each image has exactly 729 valid tokens, at positions drawn for each image.
All inputs are finite; a program needn't handle non-finite values.
Results may differ from the reference program's by a relative error of at most 0.012.
Values may be sent and summed in bfloat16 or wider, within the bound.
No kernel may reach another device: no remote copies, remote signals or barrier semaphores. Data moves between devices by JAX's collectives and lax.ppermute only.
A program may use at most 320 MiB of HBM per device.

```python
import math
import jax
import jax.numpy as jnp
from jax import lax

D = 1152
H = 16
HD = 72
FF = 4304
SEQ = 768
VALID = 729
STEP = 4
IMAGES = 16


def draw_token_mask(key, part):
    image_keys = jax.random.split(key, IMAGES)

    def one_image(image_key):
        order = jax.random.permutation(image_key, SEQ)
        return (order < VALID).astype(jnp.int32)
    return jax.vmap(one_image)(image_keys)


def unit_pair(key, shape):
    key_a, key_b = jax.random.split(key)
    base = jax.random.normal(key_a, shape, jnp.float32)
    noise = jax.random.normal(key_b, shape, jnp.float32)
    return (base, noise)


def draw_attn_params(key, part):
    shape = (D, 4 * D + 5)
    base, noise = unit_pair(jax.random.fold_in(key, 11), shape)
    spread = jax.random.uniform(jax.random.fold_in(key, 12), shape, jnp.float32, 0.6, 1.4)
    inv_root = 1.0 / math.sqrt(D)
    query_part = base[:, :D] * inv_root
    key_part = noise[:, D:2 * D] * inv_root
    value_part = base[:, 2 * D:3 * D] * inv_root
    out_part = base[:, 3 * D:4 * D] * (4.0 * inv_root)
    gain_part = spread[:, 4 * D:4 * D + 1]
    bias_part = 0.5 * base[:, 4 * D + 1:]
    return jnp.concatenate([query_part, key_part, value_part, out_part, gain_part, bias_part], axis=1)


def draw_feed_params(key, part):
    shape = (D, 2 * FF + 3)
    base, noise = unit_pair(jax.random.fold_in(key, 21), shape)
    spread = jax.random.uniform(jax.random.fold_in(key, 22), shape, jnp.float32, 0.6, 1.4)
    up_part = base[:, :FF] * (1.0 / math.sqrt(D))
    down_part = noise[:, FF:2 * FF] * (1.0 / math.sqrt(FF))
    gain_part = spread[:, 2 * FF:2 * FF + 1]
    bias_part = 0.5 * base[:, 2 * FF + 1:]
    return jnp.concatenate([up_part, down_part, gain_part, bias_part], axis=1)


def level_of(own_key, shape, cuts, low, top_value):
    loudness, own = 1.0, jax.random.fold_in(own_key, 6)
    for dim, blocks in cuts:
        heights = jnp.exp(jax.random.uniform(jax.random.fold_in(own, dim), (blocks,), jnp.float32, low / len(cuts), top_value / len(cuts)))
        loudness = loudness * jnp.repeat(heights, shape[dim] // blocks).reshape([-1 if axis == dim else 1 for axis in range(len(shape))])
    return loudness


def bell_draw(stream_key, dims, deviation, reach, cuts=(), held_as=jnp.bfloat16):
    values = jax.random.normal(stream_key, dims, jnp.float32) * deviation
    if len(cuts) > 0:
        values = level_of(stream_key, dims, cuts, -0.22, 0.18) * values
    return jnp.clip(values, min=-reach, max=reach).astype(held_as)


def setup_inputs(seed: int = 0) -> dict:
    arg_keys = jax.random.split(jax.random.key(seed), 13)
    return {
        "tokens_in": bell_draw(arg_keys[0], (IMAGES, SEQ, D), 1.0, 6.0, ((0, 16), (1, 2))),
        "cotangent": bell_draw(arg_keys[1], (IMAGES, SEQ, D), 1.0, 6.0, ((0, 16), (1, 2)), jnp.float32),
        "token_mask": draw_token_mask(jax.random.fold_in(arg_keys[12], 71), 0),
        "attn_params": draw_attn_params(jax.random.fold_in(arg_keys[12], 71), 0),
        "attn_first": bell_draw(arg_keys[4], (D, 4 * D + 5), 10.0, 60.0, ((0, 32),), jnp.float32),
        "attn_second": jnp.clip(jnp.exp(math.log(100.0) - 4.6051702 * jax.random.uniform(arg_keys[5], (D, 4 * D + 5), jnp.float32) ** level_of(arg_keys[5], (D, 4 * D + 5), ((0, 32),), -0.2, 0.2)), 1.0, 100.0),
        "feed_params": draw_feed_params(jax.random.fold_in(arg_keys[12], 71), 0),
        "feed_first": bell_draw(arg_keys[7], (D, 2 * FF + 3), 10.0, 60.0, ((0, 32),), jnp.float32),
        "feed_second": jnp.clip(jnp.exp(math.log(100.0) - 4.6051702 * jax.random.uniform(arg_keys[8], (D, 2 * FF + 3), jnp.float32) ** level_of(arg_keys[8], (D, 2 * FF + 3), ((0, 32),), -0.2, 0.2)), 1.0, 100.0),
        "up_bias": bell_draw(arg_keys[9], (FF,), 0.5, 3.0, (), jnp.float32),
        "up_bias_first": bell_draw(arg_keys[10], (FF,), 10.0, 60.0, (), jnp.float32),
        "up_bias_second": jnp.clip(jnp.exp(jax.random.uniform(arg_keys[11], (FF,), jnp.float32, math.log(1.0), math.log(100.0))), 1.0, 100.0),
    }


eps_norm = 1e-06
lr_rate = 0.01
beta_one = 0.9
beta_two = 0.999
eps_adam = 1e-08
decay_rate = 0.05

def gelu_tanh(values):
    return jax.nn.gelu(values, approximate=True)

def norm_forward(values, gain, shift):
    mean_val = lax.optimization_barrier(jnp.mean(values, axis=-1, keepdims=True))
    centred = values - mean_val
    var_val = lax.optimization_barrier(jnp.mean(centred * centred, axis=-1, keepdims=True))
    inv_std = lax.rsqrt(var_val + eps_norm)
    normed = centred * inv_std
    return (normed, inv_std, (normed * gain + shift).astype(jnp.bfloat16))

def norm_backward(grad_out, normed, inv_std, gain):
    scaled = grad_out * gain
    return inv_std * (scaled - lax.optimization_barrier(jnp.mean(scaled, axis=-1, keepdims=True)) - normed * lax.optimization_barrier(jnp.mean(scaled * normed, axis=-1, keepdims=True)))

def head_scores(query_heads, key_heads, valid):
    raw = jnp.einsum('qhd,khd->hqk', query_heads.astype(jnp.float32), key_heads.astype(jnp.float32))
    raw = raw * (1.0 / math.sqrt(HD))
    return jnp.where(valid[None, None, :], raw, -1e+30)

def adamw_step(param, first, second, grad):
    first_new = beta_one * first + (1.0 - beta_one) * grad
    second_new = beta_two * second + (1.0 - beta_two) * grad * grad
    first_hat = first_new / (1.0 - beta_one ** STEP)
    second_hat = second_new / (1.0 - beta_two ** STEP)
    param_new = param - lr_rate * (first_hat / (jnp.sqrt(second_hat) + eps_adam) + decay_rate * param)
    return (param_new, first_new, second_new)

def reference(tokens_in, cotangent, token_mask, attn_params, attn_first, attn_second, feed_params, feed_first, feed_second, up_bias, up_bias_first, up_bias_second):
    width = tokens_in.shape[-1]
    hidden = up_bias.shape[0]
    seq_len = tokens_in.shape[1]
    attn_half = lax.optimization_barrier(attn_params.astype(jnp.bfloat16))
    feed_half = lax.optimization_barrier(feed_params.astype(jnp.bfloat16))
    bias_up = lax.optimization_barrier(up_bias.astype(jnp.bfloat16)).astype(jnp.float32)
    proj_w = attn_half[:, :3 * width]
    out_w = attn_half[:, 3 * width:4 * width]
    attn_vec = attn_half[:, 4 * width:].astype(jnp.float32)
    feed_in = feed_half[:, :hidden]
    feed_out = feed_half[:, hidden:2 * hidden]
    feed_vec = feed_half[:, 2 * hidden:].astype(jnp.float32)

    def one_image(carry, item):
        image_in, image_cot, image_mask = item
        rows_in = image_in.astype(jnp.float32)
        norm_one, scale_one, half_one = norm_forward(rows_in, attn_vec[:, 0], attn_vec[:, 1])
        proj_sum = jnp.dot(half_one, proj_w, preferred_element_type=jnp.float32)
        query_half = (proj_sum[:, :width] + attn_vec[:, 2]).astype(jnp.bfloat16)
        key_half = proj_sum[:, width:2 * width].astype(jnp.bfloat16)
        value_half = (proj_sum[:, 2 * width:] + attn_vec[:, 3]).astype(jnp.bfloat16)
        query_heads = query_half.reshape(seq_len, H, HD)
        key_heads = key_half.reshape(seq_len, H, HD)
        value_heads = value_half.reshape(seq_len, H, HD)
        valid = image_mask > 0
        scores = head_scores(query_heads, key_heads, valid)
        row_max = lax.optimization_barrier(jnp.max(scores, axis=-1, keepdims=True))
        log_total = row_max + jnp.log(lax.optimization_barrier(jnp.sum(jnp.exp(scores - row_max), axis=-1, keepdims=True)))
        prob_half = jnp.exp(scores - log_total).astype(jnp.bfloat16)
        mixed_rows = jnp.einsum('hqk,khd->qhd', prob_half.astype(jnp.float32), value_heads.astype(jnp.float32)).reshape(seq_len, width).astype(jnp.bfloat16)
        resid_one = rows_in + jnp.dot(mixed_rows, out_w.T, preferred_element_type=jnp.float32) + attn_vec[:, 4]
        norm_two, scale_two, half_two = norm_forward(resid_one, feed_vec[:, 0], feed_vec[:, 1])
        pre_act = jnp.dot(half_two, feed_in, preferred_element_type=jnp.float32) + bias_up
        act_half = gelu_tanh(pre_act).astype(jnp.bfloat16)
        block_rows = resid_one + jnp.dot(act_half, feed_out.T, preferred_element_type=jnp.float32) + feed_vec[:, 2]
        grad_rows = image_cot * image_mask.astype(jnp.float32)[:, None]
        grad_half = grad_rows.astype(jnp.bfloat16)
        grad_act = jnp.dot(grad_half, feed_out, preferred_element_type=jnp.float32)
        grad_pre = jax.vjp(gelu_tanh, pre_act)[1](grad_act)[0]
        grad_pre_half = grad_pre.astype(jnp.bfloat16)
        grad_norm_two = jnp.dot(grad_pre_half, feed_in.T, preferred_element_type=jnp.float32)
        grad_resid = grad_rows + norm_backward(grad_norm_two, norm_two, scale_two, feed_vec[:, 0])
        grad_resid_half = grad_resid.astype(jnp.bfloat16)
        grad_mixed = jnp.dot(grad_resid_half, out_w, preferred_element_type=jnp.float32).astype(jnp.bfloat16)
        grad_heads = grad_mixed.reshape(seq_len, H, HD).astype(jnp.float32)
        mixed_heads = mixed_rows.reshape(seq_len, H, HD).astype(jnp.float32)
        prob_full = jnp.exp(scores - log_total)
        grad_prob = jnp.einsum('qhd,khd->hqk', grad_heads, value_heads.astype(jnp.float32))
        delta = jnp.einsum('qhd,qhd->hq', grad_heads, mixed_heads)[:, :, None]
        grad_score = (prob_full * (grad_prob - delta)).astype(jnp.bfloat16).astype(jnp.float32)
        grad_query = jnp.einsum('hqk,khd->qhd', grad_score, key_heads.astype(jnp.float32)).reshape(seq_len, width) * (1.0 / math.sqrt(HD))
        grad_key = jnp.einsum('hqk,qhd->khd', grad_score, query_heads.astype(jnp.float32)).reshape(seq_len, width) * (1.0 / math.sqrt(HD))
        grad_value = jnp.einsum('hqk,qhd->khd', prob_half.astype(jnp.float32), grad_heads).reshape(seq_len, width)
        grad_proj = jnp.concatenate([grad_query, grad_key, grad_value], axis=1)
        grad_proj_half = grad_proj.astype(jnp.bfloat16)
        grad_norm_one = jnp.dot(grad_proj_half, proj_w.T, preferred_element_type=jnp.float32)
        grad_rows_in = grad_resid + norm_backward(grad_norm_one, norm_one, scale_one, attn_vec[:, 0])
        attn_cols = jnp.stack([lax.optimization_barrier(jnp.sum(grad_norm_one * norm_one, axis=0)), lax.optimization_barrier(jnp.sum(grad_norm_one, axis=0)), lax.optimization_barrier(jnp.sum(grad_query, axis=0)), lax.optimization_barrier(jnp.sum(grad_value, axis=0)), lax.optimization_barrier(jnp.sum(grad_resid, axis=0))], axis=1)
        feed_cols = jnp.stack([lax.optimization_barrier(jnp.sum(grad_norm_two * norm_two, axis=0)), lax.optimization_barrier(jnp.sum(grad_norm_two, axis=0)), lax.optimization_barrier(jnp.sum(grad_rows, axis=0))], axis=1)
        acc_proj, acc_out, acc_in, acc_down, acc_attn_cols, acc_feed_cols, acc_up = carry
        acc_proj = acc_proj + jnp.dot(half_one.T, grad_proj_half, preferred_element_type=jnp.float32)
        acc_out = acc_out + jnp.dot(grad_resid_half.T, mixed_rows, preferred_element_type=jnp.float32)
        acc_in = acc_in + jnp.dot(half_two.T, grad_pre_half, preferred_element_type=jnp.float32)
        acc_down = acc_down + jnp.dot(grad_half.T, act_half, preferred_element_type=jnp.float32)
        acc_attn_cols = acc_attn_cols + attn_cols
        acc_feed_cols = acc_feed_cols + feed_cols
        acc_up = acc_up + lax.optimization_barrier(jnp.sum(grad_pre, axis=0))
        return ((acc_proj, acc_out, acc_in, acc_down, acc_attn_cols, acc_feed_cols, acc_up), (block_rows, grad_rows_in))
    start_carry = (jnp.zeros((width, 3 * width), jnp.float32), jnp.zeros((width, width), jnp.float32), jnp.zeros((width, hidden), jnp.float32), jnp.zeros((width, hidden), jnp.float32), jnp.zeros((width, 5), jnp.float32), jnp.zeros((width, 3), jnp.float32), jnp.zeros((hidden,), jnp.float32))
    totals, outputs = lax.scan(one_image, start_carry, (tokens_in, cotangent, token_mask))
    block_out, grad_input = outputs
    acc_proj, acc_out, acc_in, acc_down, acc_attn_cols, acc_feed_cols, acc_up = totals
    grad_attn = jnp.concatenate([acc_proj, acc_out, acc_attn_cols], axis=1)
    grad_feed = jnp.concatenate([acc_in, acc_down, acc_feed_cols], axis=1)
    new_attn, new_attn_first, new_attn_second = adamw_step(attn_params, attn_first, attn_second, grad_attn)
    new_feed, new_feed_first, new_feed_second = adamw_step(feed_params, feed_first, feed_second, grad_feed)
    new_up, new_up_first, new_up_second = adamw_step(up_bias, up_bias_first, up_bias_second, acc_up)
    return (block_out, grad_input, grad_attn, grad_feed, acc_up, new_attn, new_attn_first, new_attn_second, new_feed, new_feed_first, new_feed_second, new_up, new_up_first, new_up_second)
```

```python
import math

import jax
import jax.numpy as jnp
from jax import lax
from jax.sharding import PartitionSpec as P

H = 16
HD = 72
STEP = 4


eps_norm = 1e-06
lr_rate = 0.01
beta_one = 0.9
beta_two = 0.999
eps_adam = 1e-08
decay_rate = 0.05

bf16 = jnp.bfloat16
f32 = jnp.float32


def gelu_tanh(values):
    return jax.nn.gelu(values, approximate=True)


def norm_stats(values):
    mean_val = jnp.mean(values, axis=-1, keepdims=True)
    centred = values - mean_val
    var_val = jnp.mean(centred * centred, axis=-1, keepdims=True)
    inv_std = lax.rsqrt(var_val + eps_norm)
    return centred * inv_std, inv_std


def norm_backward(grad_out, normed, inv_std, gain):
    scaled = grad_out * gain
    return inv_std * (
        scaled
        - jnp.mean(scaled, axis=-1, keepdims=True)
        - normed * jnp.mean(scaled * normed, axis=-1, keepdims=True)
    )


def adamw_step(param, first, second, grad):
    first_new = beta_one * first + (1.0 - beta_one) * grad
    second_new = beta_two * second + (1.0 - beta_two) * grad * grad
    first_hat = first_new / (1.0 - beta_one**STEP)
    second_hat = second_new / (1.0 - beta_two**STEP)
    param_new = param - lr_rate * (
        first_hat / (jnp.sqrt(second_hat) + eps_adam) + decay_rate * param
    )
    return (param_new, first_new, second_new)


def mm(left, right):
    return jnp.dot(left, right, preferred_element_type=f32)


def mm_nt(left, right):
    return lax.dot_general(left, right, (((1,), (1,)), ((), ())), preferred_element_type=f32)


def mm_tn(left, right):
    return lax.dot_general(left, right, (((0,), (0,)), ((), ())), preferred_element_type=f32)


def dp_swap(value, mask):
    count = lax.axis_size("dp")
    return lax.ppermute(value, "dp", [(i, i ^ mask) for i in range(count)])


def core_swap(value):
    return dp_swap(value, 1)


def x_swap(value):
    return dp_swap(value, 2)


def z_swap(value, step):
    return dp_swap(value, 4 * step)


def y_swap(value):
    count = lax.axis_size("ctx")
    return lax.ppermute(value, "ctx", [(i, i ^ 1) for i in range(count)])


def gather_line(block, depth):
    return [block] + [z_swap(block, step) for step in range(1, depth)]


def gather_plane(line):
    whole = jnp.concatenate(line, axis=0)
    half = whole.shape[0] // 2
    over_x = x_swap(whole)
    over_y = y_swap(whole)
    corner_a = y_swap(over_x[:half])
    corner_b = x_swap(over_y[half:])
    return jnp.concatenate([whole, over_x, over_y, corner_a, corner_b], axis=0)


def add_half(left, right):
    return (left.astype(f32) + right.astype(f32)).astype(bf16)


def scatter_sum(chunks, depth):
    near, side_x, side_y, corner = chunks
    half = near.shape[0] // 2
    from_y = y_swap(corner[:half])
    from_x = x_swap(corner[half:])
    side_x = jnp.concatenate([add_half(side_x[:half], from_y), side_x[half:]], axis=0)
    side_y = jnp.concatenate([side_y[:half], add_half(side_y[half:], from_x)], axis=0)
    got_x = x_swap(side_x)
    got_y = y_swap(side_y)
    total = (near.astype(f32) + got_x.astype(f32) + got_y.astype(f32)).astype(bf16)
    rows = total.shape[0] // depth
    out = total[:rows].astype(f32)
    for step in range(1, depth):
        out = out + z_swap(total[step * rows : (step + 1) * rows], step).astype(f32)
    return out


def weight_chunks(left, right):
    size = left.shape[1] // 4
    return [mm_tn(left[:, i * size : (i + 1) * size], right).astype(bf16) for i in range(4)]


def split_three(values):
    high = lax.reduce_precision(values, 8, 7)
    rest = values - high
    mid = lax.reduce_precision(rest, 8, 7)
    low = rest - mid
    return jnp.concatenate(
        [high.astype(bf16), mid.astype(bf16), low.astype(bf16)], axis=1
    )


def head_scores(query_heads, key_heads, valid):
    raw = jnp.einsum("bqhd,bkhd->bhqk", query_heads, key_heads, preferred_element_type=f32)
    raw = raw * (1.0 / math.sqrt(HD))
    return jnp.where(valid[:, None, None, :], raw, -1e30)


def attend(query, key, value, valid):
    images, rows, width = query.shape
    heads = width // HD
    q_heads = query.reshape(images, rows, heads, HD)
    k_heads = key.reshape(images, -1, heads, HD)
    v_heads = value.reshape(images, -1, heads, HD)
    scores = head_scores(q_heads, k_heads, valid)
    row_max = jnp.max(scores, axis=-1, keepdims=True)
    log_total = row_max + jnp.log(jnp.sum(jnp.exp(scores - row_max), axis=-1, keepdims=True))
    prob = jnp.exp(scores - log_total).astype(bf16)
    mixed = jnp.einsum("bhqk,bkhd->bqhd", prob, v_heads, preferred_element_type=f32)
    return mixed.reshape(images, rows, width).astype(bf16), log_total


def attend_back(query, key, value, valid, mixed, log_total, grad_mixed):
    images, rows, width = query.shape
    heads = width // HD
    keys = key.shape[1]
    q_heads = query.reshape(images, rows, heads, HD)
    k_heads = key.reshape(images, keys, heads, HD)
    v_heads = value.reshape(images, keys, heads, HD)
    g_heads = grad_mixed.reshape(images, rows, heads, HD)
    o_heads = mixed.reshape(images, rows, heads, HD)
    scores = head_scores(q_heads, k_heads, valid)
    prob = jnp.exp(scores - log_total)
    prob_half = prob.astype(bf16)
    grad_prob = jnp.einsum("bqhd,bkhd->bhqk", g_heads, v_heads, preferred_element_type=f32)
    delta = jnp.einsum("bqhd,bqhd->bhq", g_heads.astype(f32), o_heads.astype(f32))[..., None]
    grad_score = (prob * (grad_prob - delta)).astype(bf16)
    scale = 1.0 / math.sqrt(HD)
    grad_q = jnp.einsum("bhqk,bkhd->bqhd", grad_score, k_heads, preferred_element_type=f32)
    grad_k = jnp.einsum("bhqk,bqhd->bkhd", grad_score, q_heads, preferred_element_type=f32)
    grad_v = jnp.einsum("bhqk,bqhd->bkhd", prob_half, g_heads, preferred_element_type=f32)
    return (
        grad_q.reshape(images, rows, width) * scale,
        grad_k.reshape(images, keys, width) * scale,
        grad_v.reshape(images, keys, width),
    )


def body(
    tokens_in,
    cotangent,
    token_mask,
    attn_params,
    attn_first,
    attn_second,
    feed_params,
    feed_first,
    feed_second,
    up_bias,
    up_bias_first,
    up_bias_second,
):
    images, local_len, width = tokens_in.shape
    hidden = up_bias.shape[0]
    owned = attn_params.shape[0]
    dp_count = lax.axis_size("dp")
    ctx_count = lax.axis_size("ctx")
    assert images == 1 and ctx_count == 2 and dp_count % 4 == 0
    depth = dp_count // 4
    dp_at = lax.axis_index("dp")
    y_at = lax.axis_index("ctx")
    core = dp_at % 2
    x_at = (dp_at // 2) % 2
    z_at = dp_at // 4
    first_core = core == 0
    half_w = width // 2
    half_h = hidden // 2

    block = 2 * owned
    spot = jnp.arange(width, dtype=jnp.int32)
    place = spot // block
    y_of = y_at ^ (place // (2 * depth))
    x_of = x_at ^ ((place // depth) % 2)
    z_of = z_at ^ (place % depth)
    core_of = (spot % block) // owned
    natural = (((z_of * 2 + x_of) * 2 + core_of) * 2 + y_of) * owned + spot % owned
    row_ids = lax.broadcasted_iota(jnp.int32, (3 * width, width), 0) % width
    order_three = (row_ids == natural[None, :]).astype(bf16)
    order = order_three[:width]

    def to_local(values):
        return mm(split_three(values), order_three)

    order_back = jnp.tile(order.T, (3, 1))

    def to_natural(values):
        return mm(split_three(values), order_back)

    rows_own = tokens_in[0]
    rows_far = y_swap(rows_own)
    mask_own = token_mask.astype(f32)
    mask_img = jnp.concatenate([mask_own, y_swap(mask_own)], axis=1)
    mask_all = jnp.concatenate([mask_img, core_swap(mask_img)], axis=0)
    valid = mask_all > 0

    attn_half = attn_params.astype(bf16)
    feed_half = feed_params.astype(bf16)

    def pick(at):
        parts = [
            attn_half[:, i * width + at * half_w : i * width + (at + 1) * half_w]
            for i in range(4)
        ]
        parts.append(attn_half[:, 4 * width :])
        parts.append(feed_half[:, 2 * hidden :])
        for i in range(2):
            parts.append(feed_half[:, i * hidden + at * half_h : i * hidden + (at + 1) * half_h])
        return jnp.concatenate(parts, axis=1)

    part_zero, part_one = pick(0), pick(1)
    keep = jnp.where(first_core, part_zero, part_one)
    give = jnp.where(first_core, part_one, part_zero)
    got = core_swap(give)
    shard = jnp.concatenate(
        [jnp.where(first_core, keep, got), jnp.where(first_core, got, keep)], axis=0
    )
    vecs = attn_params.shape[1] - 4 * width + feed_params.shape[1] - 2 * hidden
    cut_a = 2 * half_w
    cut_b = 4 * half_w + vecs
    line_a = gather_line(shard[:, :cut_a], depth)
    line_b = gather_line(shard[:, cut_a:cut_b], depth)
    shard_c, line_a = lax.optimization_barrier((shard[:, cut_b : cut_b + half_h], line_a))
    line_c = gather_line(shard_c, depth)
    shard_d, line_b = lax.optimization_barrier((shard[:, cut_b + half_h :], line_b))
    line_d = gather_line(shard_d, depth)
    w_qk = gather_plane(line_a)
    w_vo = gather_plane(line_b)
    w_up = gather_plane(line_c)
    w_down = gather_plane(line_d)
    w_q, w_k = w_qk[:, :half_w], w_qk[:, half_w:]
    w_v, w_o = w_vo[:, :half_w], w_vo[:, half_w : 2 * half_w]
    vec = w_vo[:, 2 * half_w :]
    vec_nat = mm(order, vec[:, 2:4])
    vec_t = vec.astype(f32).T
    gain_one, shift_one, bias_o = vec_t[0], vec_t[1], vec_t[4]
    gain_two, shift_two, bias_d = vec_t[5], vec_t[6], vec_t[7]
    bias_qv = jnp.where(first_core, vec_nat[:half_w], vec_nat[half_w:]).T
    bias_up = lax.optimization_barrier(up_bias.astype(bf16)).astype(f32)
    bias_up = jnp.where(first_core, bias_up[:half_h], bias_up[half_h:])

    live = mask_own.reshape(local_len, 1)
    grad_rows = to_local(cotangent[0] * live)
    grad_half = grad_rows.astype(bf16)
    grad_both = jnp.concatenate([grad_half, core_swap(grad_half)], axis=0)

    rows_img = mm(jnp.concatenate([rows_own, rows_far], axis=0), order)
    rows_in = rows_img[:local_len]
    norm_img, scale_img = norm_stats(rows_img)
    half_img = (norm_img * gain_one + shift_one).astype(bf16)
    half_far = core_swap(half_img)
    one_all = jnp.concatenate([half_img, half_far], axis=0)
    one_own = jnp.concatenate([half_img[:local_len], half_far[:local_len]], axis=0)
    seq = 2 * local_len
    query = (mm(one_own, w_q) + bias_qv[0]).astype(bf16).reshape(2, local_len, half_w)
    key = mm(one_all, w_k).astype(bf16).reshape(2, seq, half_w)
    value = (mm(one_all, w_v) + bias_qv[1]).astype(bf16).reshape(2, seq, half_w)
    mixed, log_total = attend(query, key, value, valid)
    mixed_rows = mixed.reshape(2 * local_len, half_w)
    part = mm_nt(mixed_rows, w_o)
    resid = rows_in + part[:local_len] + core_swap(part[local_len:]) + bias_o

    norm_two, scale_two = norm_stats(resid)
    half_two = (norm_two * gain_two + shift_two).astype(bf16)
    two_both = jnp.concatenate([half_two, core_swap(half_two)], axis=0)
    pre_act = mm(two_both, w_up) + bias_up
    act_half = gelu_tanh(pre_act).astype(bf16)
    down_sum = scatter_sum(weight_chunks(grad_both, act_half), depth)
    grad_act = mm(grad_both, w_down)
    grad_pre = jax.vjp(gelu_tanh, pre_act)[1](grad_act)[0]
    grad_pre_half = grad_pre.astype(bf16)
    up_sum = scatter_sum(weight_chunks(two_both, grad_pre_half), depth)
    part = mm_nt(act_half, w_down)
    block_rows = resid + part[:local_len] + core_swap(part[local_len:]) + bias_d
    block_out = to_natural(block_rows)[None]

    part = mm_nt(grad_pre_half, w_up)
    grad_norm_two = part[:local_len] + core_swap(part[local_len:])
    grad_resid = grad_rows + norm_backward(grad_norm_two, norm_two, scale_two, gain_two)
    grad_resid_half = grad_resid.astype(bf16)
    resid_both = jnp.concatenate([grad_resid_half, core_swap(grad_resid_half)], axis=0)

    grad_mixed = mm(resid_both, w_o).astype(bf16).reshape(2, local_len, half_w)
    grad_q, grad_k, grad_v = attend_back(
        query, key, value, valid, mixed, log_total, grad_mixed
    )
    grad_q = grad_q.reshape(2 * local_len, half_w)
    grad_k = grad_k.reshape(2 * seq, half_w)
    grad_v = grad_v.reshape(2 * seq, half_w)
    grad_q_half = grad_q.astype(bf16)
    grad_k_half = grad_k.astype(bf16)
    grad_v_half = grad_v.astype(bf16)
    part_q = mm_nt(grad_q_half, w_q).reshape(2, local_len, width)
    part_kv = (mm_nt(grad_k_half, w_k) + mm_nt(grad_v_half, w_v)).reshape(2, seq, width)
    part_own = jnp.concatenate([part_q[0] + part_kv[0, :local_len], part_kv[0, local_len:]], axis=0)
    part_sib = jnp.concatenate([part_q[1] + part_kv[1, :local_len], part_kv[1, local_len:]], axis=0)
    part_img = part_own + core_swap(part_sib)
    part_far = part_img[local_len:].astype(bf16)
    part_far = y_swap(jnp.concatenate([part_far[:, half_w:], part_far[:, :half_w]], axis=1))
    grad_norm_one = part_img[:local_len] + part_far.astype(f32)
    grad_in = grad_resid + norm_backward(
        grad_norm_one, norm_img[:local_len], scale_img[:local_len], gain_one
    )
    grad_input = to_natural(grad_in)[None]

    zeros = jnp.zeros((half_w,), f32)
    sum_q = jnp.sum(grad_q, axis=0)
    sum_v = jnp.sum(grad_v, axis=0)

    def spread(vector):
        return jnp.where(
            first_core,
            jnp.concatenate([vector, zeros]),
            jnp.concatenate([zeros, vector]),
        )

    both = to_local(jnp.stack([spread(sum_q), spread(sum_v)], axis=0))
    cols = jnp.stack(
        [
            jnp.sum(part_img * norm_img, axis=0),
            jnp.sum(part_img, axis=0),
            both[0],
            both[1],
            jnp.sum(grad_resid, axis=0),
            jnp.sum(grad_norm_two * norm_two, axis=0),
            jnp.sum(grad_norm_two, axis=0),
            jnp.sum(grad_rows, axis=0),
        ],
        axis=1,
    ).astype(bf16)
    size = width // 4
    chunks_q = weight_chunks(one_own, grad_q_half)
    chunks_k = weight_chunks(one_all, grad_k_half)
    chunks_v = weight_chunks(one_all, grad_v_half)
    chunks_o = weight_chunks(resid_both, mixed_rows)
    chunks_qk = [jnp.concatenate([chunks_q[i], chunks_k[i]], axis=1) for i in range(4)]
    chunks_vo = [
        jnp.concatenate([chunks_v[i], chunks_o[i], cols[i * size : (i + 1) * size]], axis=1)
        for i in range(4)
    ]
    qk_sum = scatter_sum(chunks_qk, depth)
    vo_sum = scatter_sum(chunks_vo, depth)

    def trade(values):
        upper, lower = values[:owned], values[owned:]
        mine = jnp.where(first_core, upper, lower)
        other = core_swap(jnp.where(first_core, lower, upper))
        return mine, other

    def join(mine, other):
        return jnp.where(
            first_core,
            jnp.concatenate([mine, other], axis=1),
            jnp.concatenate([other, mine], axis=1),
        )

    down_mine, down_other = trade(down_sum)
    up_mine, up_other = trade(up_sum)
    qk_mine, qk_other = trade(qk_sum)
    vo_mine, vo_other = trade(vo_sum)
    vec_sum = vo_mine[:, 2 * half_w :] + vo_other[:, 2 * half_w :]
    grad_attn = jnp.concatenate(
        [
            join(qk_mine[:, :half_w], qk_other[:, :half_w]),
            join(qk_mine[:, half_w:], qk_other[:, half_w:]),
            join(vo_mine[:, :half_w], vo_other[:, :half_w]),
            join(vo_mine[:, half_w : 2 * half_w], vo_other[:, half_w : 2 * half_w]),
            vec_sum[:, :5],
        ],
        axis=1,
    )
    grad_feed = jnp.concatenate(
        [join(up_mine, up_other), join(down_mine, down_other), vec_sum[:, 5:]], axis=1
    )
    bias_sum = jnp.sum(grad_pre, axis=0, keepdims=True)
    bias_sum = bias_sum + y_swap(bias_sum)
    mask = 2
    while mask < dp_count:
        bias_sum = bias_sum + dp_swap(bias_sum, mask)
        mask *= 2
    grad_up = join(bias_sum, core_swap(bias_sum)).reshape(hidden)

    new_attn, new_attn_first, new_attn_second = adamw_step(
        attn_params, attn_first, attn_second, grad_attn
    )
    new_feed, new_feed_first, new_feed_second = adamw_step(
        feed_params, feed_first, feed_second, grad_feed
    )
    new_up, new_up_first, new_up_second = adamw_step(
        up_bias, up_bias_first, up_bias_second, grad_up
    )
    return (
        block_out,
        grad_input,
        grad_attn,
        grad_feed,
        grad_up,
        new_attn,
        new_attn_first,
        new_attn_second,
        new_feed,
        new_feed_first,
        new_feed_second,
        new_up,
        new_up_first,
        new_up_second,
    )


def solution(mesh):
    tokens = P("dp", "ctx", None)
    params = P(("dp", "ctx"), None)
    return jax.shard_map(
        body,
        mesh=mesh,
        in_specs=(tokens, tokens, P("dp", "ctx")) + (params,) * 6 + (P(),) * 3,
        out_specs=(tokens, tokens, params, params, P()) + (params,) * 6 + (P(),) * 3,
        check_vma=False,
    )
```

```python
import math

import jax
import jax.numpy as jnp
from jax import lax
from jax.sharding import PartitionSpec as P


HD = 72
STEP = 4


eps_norm = 1e-06
lr_rate = 0.01
beta_one = 0.9
beta_two = 0.999
eps_adam = 1e-08
decay_rate = 0.05

bf16 = jnp.bfloat16
f32 = jnp.float32


def gelu_tanh(values):
    return jax.nn.gelu(values, approximate=True)


def norm_stats(values):
    mean_val = jnp.mean(values, axis=-1, keepdims=True)
    centred = values - mean_val
    var_val = jnp.mean(centred * centred, axis=-1, keepdims=True)
    inv_std = lax.rsqrt(var_val + eps_norm)
    return centred * inv_std, inv_std


def norm_backward(grad_out, normed, inv_std, gain):
    scaled = grad_out * gain
    return inv_std * (
        scaled
        - jnp.mean(scaled, axis=-1, keepdims=True)
        - normed * jnp.mean(scaled * normed, axis=-1, keepdims=True)
    )


def adamw_step(param, first, second, grad):
    first_new = beta_one * first + (1.0 - beta_one) * grad
    second_new = beta_two * second + (1.0 - beta_two) * grad * grad
    first_hat = first_new / (1.0 - beta_one**STEP)
    second_hat = second_new / (1.0 - beta_two**STEP)
    param_new = param - lr_rate * (
        first_hat / (jnp.sqrt(second_hat) + eps_adam) + decay_rate * param
    )
    return (param_new, first_new, second_new)


def mm(left, right):
    return jnp.dot(left, right, preferred_element_type=f32)


def mm_nt(left, right):
    return lax.dot_general(left, right, (((1,), (1,)), ((), ())), preferred_element_type=f32)


def mm_tn(left, right):
    return lax.dot_general(left, right, (((0,), (0,)), ((), ())), preferred_element_type=f32)


def dp_swap(value, mask):
    count = lax.axis_size("dp")
    return lax.ppermute(value, "dp", [(i, i ^ mask) for i in range(count)])


def core_swap(value):
    return dp_swap(value, 1)


def x_swap(value):
    return dp_swap(value, 2)


def z_swap(value, step):
    return dp_swap(value, 4 * step)


def y_swap(value):
    count = lax.axis_size("ctx")
    return lax.ppermute(value, "ctx", [(i, i ^ 1) for i in range(count)])


def after(value, *others):
    return lax.optimization_barrier((value, others))[0]


def gather_line(block, depth):
    return [block] + [z_swap(block, step) for step in range(1, depth)]


def gather_sides(line, *others):
    whole = after(jnp.concatenate(line, axis=0), *others)
    return whole, x_swap(whole), y_swap(whole)


def gather_corner(sides, *others):
    whole, over_x, over_y = sides
    half = whole.shape[0] // 2
    send_x, send_y = after((over_x[:half], over_y[half:]), *others)
    return [whole, over_x, over_y, y_swap(send_x), x_swap(send_y)]


def gather_all(pieces):
    return jnp.concatenate(pieces, axis=0)


def add_half(left, right):
    return (left.astype(f32) + right.astype(f32)).astype(bf16)


def scatter_corner(corner, cut):
    split = corner.shape[0] * cut // 2
    from_y = y_swap(corner[:split]) if cut > 0 else None
    from_x = x_swap(corner[split:]) if cut < 2 else None
    return from_y, from_x


def scatter_sides(chunks, corners, *others):
    near, side_x, side_y = chunks
    from_y, from_x = after(corners, *others)
    if from_y is not None:
        split = from_y.shape[0]
        side_x = jnp.concatenate([add_half(side_x[:split], from_y), side_x[split:]], axis=0)
    if from_x is not None:
        split = near.shape[0] - from_x.shape[0]
        side_y = jnp.concatenate([side_y[:split], add_half(side_y[split:], from_x)], axis=0)
    return near, x_swap(side_x), y_swap(side_y)


def scatter_line(sides, depth, *others):
    near, got_x, got_y = after(sides, *others)
    total = (near.astype(f32) + got_x.astype(f32) + got_y.astype(f32)).astype(bf16)
    rows = total.shape[0] // depth
    parts = [total[step * rows : (step + 1) * rows] for step in range(depth)]
    return parts[:1] + [z_swap(parts[step], step) for step in range(1, depth)]


def scatter_done(parts, *others):
    parts = after(parts, *others)
    out = parts[0].astype(f32)
    for part in parts[1:]:
        out = out + part.astype(f32)
    return out


def weight_chunks(left, right):
    size = left.shape[1] // 4
    return [mm_tn(left[:, i * size : (i + 1) * size], right).astype(bf16) for i in range(3)]


def weight_corner(left, right):
    size = left.shape[1] // 4
    return mm_tn(left[:, 3 * size :], right).astype(bf16)


def split_two(values):
    high = lax.reduce_precision(values, 8, 7)
    return jnp.concatenate([high.astype(bf16), (values - high).astype(bf16)], axis=1)


def head_scores(query_heads, key_heads, valid):
    raw = jnp.einsum("bqhd,bkhd->bhqk", query_heads, key_heads, preferred_element_type=f32)
    raw = raw * (1.0 / math.sqrt(HD))
    return jnp.where(valid[:, None, None, :], raw, -1e30)


def attend(query, key, value, valid):
    images, rows, width = query.shape
    heads = width // HD
    q_heads = query.reshape(images, rows, heads, HD)
    k_heads = key.reshape(images, -1, heads, HD)
    v_heads = value.reshape(images, -1, heads, HD)
    scores = head_scores(q_heads, k_heads, valid)
    row_max = jnp.max(scores, axis=-1, keepdims=True)
    log_total = row_max + jnp.log(jnp.sum(jnp.exp(scores - row_max), axis=-1, keepdims=True))
    prob = jnp.exp(scores - log_total).astype(bf16)
    mixed = jnp.einsum("bhqk,bkhd->bqhd", prob, v_heads, preferred_element_type=f32)
    return mixed.reshape(images, rows, width).astype(bf16), log_total


def attend_back(query, key, value, valid, mixed, log_total, grad_mixed):
    images, rows, width = query.shape
    heads = width // HD
    keys = key.shape[1]
    q_heads = query.reshape(images, rows, heads, HD)
    k_heads = key.reshape(images, keys, heads, HD)
    v_heads = value.reshape(images, keys, heads, HD)
    g_heads = grad_mixed.reshape(images, rows, heads, HD)
    o_heads = mixed.reshape(images, rows, heads, HD)
    scores = head_scores(q_heads, k_heads, valid)
    prob = jnp.exp(scores - log_total)
    prob_half = prob.astype(bf16)
    grad_prob = jnp.einsum("bqhd,bkhd->bhqk", g_heads, v_heads, preferred_element_type=f32)
    delta = jnp.einsum("bqhd,bqhd->bhq", g_heads.astype(f32), o_heads.astype(f32))[..., None]
    grad_score = (prob * (grad_prob - delta)).astype(bf16)
    scale = 1.0 / math.sqrt(HD)
    grad_q = jnp.einsum("bhqk,bkhd->bqhd", grad_score, k_heads, preferred_element_type=f32)
    grad_k = jnp.einsum("bhqk,bqhd->bkhd", grad_score, q_heads, preferred_element_type=f32)
    grad_v = jnp.einsum("bhqk,bqhd->bkhd", prob_half, g_heads, preferred_element_type=f32)
    return (
        grad_q.reshape(images, rows, width) * scale,
        grad_k.reshape(images, keys, width) * scale,
        grad_v.reshape(images, keys, width),
        grad_score,
    )


def body(
    tokens_in,
    cotangent,
    token_mask,
    attn_params,
    attn_first,
    attn_second,
    feed_params,
    feed_first,
    feed_second,
    up_bias,
    up_bias_first,
    up_bias_second,
):
    images, local_len, width = tokens_in.shape
    hidden = up_bias.shape[0]
    owned = attn_params.shape[0]
    dp_count = lax.axis_size("dp")
    ctx_count = lax.axis_size("ctx")
    assert images == 1 and ctx_count == 2 and dp_count % 4 == 0
    depth = dp_count // 4
    dp_at = lax.axis_index("dp")
    y_at = lax.axis_index("ctx")
    core = dp_at % 2
    x_at = (dp_at // 2) % 2
    z_at = dp_at // 4
    first_core = core == 0
    half_w = width // 2
    half_h = hidden // 2

    rows_own = tokens_in[0]
    mask_own = token_mask.astype(f32)
    mask_img = jnp.concatenate([mask_own, y_swap(mask_own)], axis=1)
    mask_all = jnp.concatenate([mask_img, core_swap(mask_img)], axis=0)
    valid = mask_all > 0

    attn_half = attn_params.astype(bf16)
    feed_half = feed_params.astype(bf16)

    def pick(at):
        parts = [
            attn_half[:, i * width + at * half_w : i * width + (at + 1) * half_w]
            for i in range(4)
        ]
        parts.append(attn_half[:, 4 * width :])
        parts.append(feed_half[:, 2 * hidden :])
        for i in range(2):
            parts.append(feed_half[:, i * hidden + at * half_h : i * hidden + (at + 1) * half_h])
        return jnp.concatenate(parts, axis=1)

    part_zero, part_one = pick(0), pick(1)
    keep = jnp.where(first_core, part_zero, part_one)
    give = jnp.where(first_core, part_one, part_zero)
    got = core_swap(give)
    shard = jnp.concatenate(
        [jnp.where(first_core, keep, got), jnp.where(first_core, got, keep)], axis=0
    )
    vecs = attn_params.shape[1] - 4 * width + feed_params.shape[1] - 2 * hidden
    cut = 4 * half_w + vecs
    line_a = gather_line(shard[:, :cut], depth)
    sides_a = gather_sides(line_a)
    all_a = gather_corner(sides_a)
    w_attn = gather_all(all_a)
    line_c = gather_line(after(shard[:, cut : cut + half_h], *sides_a[1:]), depth)
    rows_far = y_swap(after(rows_own, shard))

    block = 2 * owned
    spot = after(jnp.arange(width, dtype=jnp.int32), shard)
    place = spot // block
    y_of = y_at ^ (place // (2 * depth))
    x_of = x_at ^ ((place // depth) % 2)
    z_of = z_at ^ (place % depth)
    core_of = (spot % block) // owned
    natural = (((z_of * 2 + x_of) * 2 + core_of) * 2 + y_of) * owned + spot % owned
    row_ids = lax.broadcasted_iota(jnp.int32, (2 * width, width), 0) % width
    order_two = (row_ids == natural[None, :]).astype(bf16)
    order = order_two[:width]

    def to_local(values):
        return mm(split_two(values), order_two)

    order_back = jnp.tile(order.T, (2, 1))

    def to_natural(values):
        return mm(split_two(values), order_back)

    w_q, w_k, w_v, w_o = (w_attn[:, i * half_w : (i + 1) * half_w] for i in range(4))
    vec = w_attn[:, 4 * half_w :]
    vec_nat = mm(order, vec[:, 2:4])
    vec_t = vec.astype(f32).T
    gain_one, shift_one, bias_o = vec_t[0], vec_t[1], vec_t[4]
    gain_two, shift_two, bias_d = vec_t[5], vec_t[6], vec_t[7]
    bias_qv = jnp.where(first_core, vec_nat[:half_w], vec_nat[half_w:]).T
    bias_up = lax.optimization_barrier(up_bias.astype(bf16)).astype(f32)
    bias_up = jnp.where(first_core, bias_up[:half_h], bias_up[half_h:])

    live = mask_own.reshape(local_len, 1)
    grad_rows = to_local(after(cotangent[0], sides_a[0]) * live)
    grad_half = grad_rows.astype(bf16)
    grad_both = jnp.concatenate([grad_half, core_swap(grad_half)], axis=0)

    rows_img = mm(after(jnp.concatenate([rows_own, rows_far], axis=0), sides_a[0]), order)
    rows_in = rows_img[:local_len]
    norm_img, scale_img = norm_stats(rows_img)
    half_img = (norm_img * gain_one + shift_one).astype(bf16)
    half_far = core_swap(half_img)
    one_all = jnp.concatenate([half_img, half_far], axis=0)
    one_own = jnp.concatenate([half_img[:local_len], half_far[:local_len]], axis=0)
    seq = 2 * local_len
    query = (mm(one_own, w_q) + bias_qv[0]).astype(bf16).reshape(2, local_len, half_w)
    key = mm(one_all, w_k).astype(bf16).reshape(2, seq, half_w)
    value = (mm(one_all, w_v) + bias_qv[1]).astype(bf16).reshape(2, seq, half_w)
    sides_c = gather_sides(line_c, query, key, value)
    line_d = gather_line(after(shard[:, cut + half_h :], *line_c), depth)
    query, key, value = after((query, key, value), sides_c[0])
    mixed, log_total = attend(query, key, value, valid)
    sides_d = gather_sides(line_d, mixed)
    all_c = gather_corner(sides_c, mixed)
    w_up = gather_all(all_c)
    mixed = after(mixed, sides_d[0], *all_c[1:3])
    mixed_rows = mixed.reshape(2 * local_len, half_w)
    part = mm_nt(mixed_rows, w_o)
    resid = rows_in + part[:local_len] + core_swap(part[local_len:]) + bias_o

    norm_two, scale_two = norm_stats(resid)
    half_two = (norm_two * gain_two + shift_two).astype(bf16)
    all_d = gather_corner(sides_d, half_two)
    w_down = gather_all(all_d)
    two_both = jnp.concatenate([half_two, core_swap(half_two)], axis=0)
    pre_act = mm(two_both, w_up) + bias_up
    act_half = gelu_tanh(pre_act).astype(bf16)
    down_corner = scatter_corner(weight_corner(grad_both, act_half), 2)
    down_chunks = weight_chunks(grad_both, act_half)
    grad_act = mm(after(grad_both, *down_chunks), w_down)
    grad_pre = jax.vjp(gelu_tanh, pre_act)[1](grad_act)[0]
    grad_pre_half = grad_pre.astype(bf16)
    up_corner = scatter_corner(weight_corner(two_both, grad_pre_half), 0)
    part = mm_nt(grad_pre_half, w_up)
    part_far = core_swap(part[local_len:])
    up_chunks = weight_chunks(two_both, after(grad_pre_half, part))
    down_sides = scatter_sides(down_chunks, down_corner, part)
    grad_norm_two = part[:local_len] + after(part_far, up_chunks)
    grad_resid = grad_rows + norm_backward(grad_norm_two, norm_two, scale_two, gain_two)
    grad_resid_half = grad_resid.astype(bf16)
    resid_far = core_swap(grad_resid_half)
    up_sides = scatter_sides(up_chunks, up_corner, grad_resid_half)
    resid_both = jnp.concatenate([grad_resid_half, resid_far], axis=0)

    grad_mixed = mm(resid_both, w_o).astype(bf16).reshape(2, local_len, half_w)
    grad_q, grad_k, grad_v, grad_score = attend_back(
        query, key, value, valid, mixed, log_total, grad_mixed
    )
    down_line = scatter_line(down_sides, depth, grad_score)
    grad_q = grad_q.reshape(2 * local_len, half_w)
    grad_k = grad_k.reshape(2 * seq, half_w)
    grad_v = grad_v.reshape(2 * seq, half_w)
    grad_q_half = grad_q.astype(bf16)
    grad_k_half = grad_k.astype(bf16)
    grad_v_half = grad_v.astype(bf16)
    corner_all = jnp.concatenate(
        [
            weight_corner(one_own, grad_q_half),
            weight_corner(one_all, grad_k_half),
            weight_corner(one_all, grad_v_half),
            weight_corner(resid_both, mixed_rows),
        ],
        axis=1,
    )
    attn_corner = scatter_corner(corner_all, 1)
    up_line = scatter_line(up_sides, depth, corner_all)
    pieces = [
        weight_chunks(one_own, grad_q_half),
        weight_chunks(one_all, grad_k_half),
        weight_chunks(one_all, grad_v_half),
        weight_chunks(resid_both, mixed_rows),
    ]
    attn_chunks = [jnp.concatenate([piece[i] for piece in pieces], axis=1) for i in range(3)]
    attn_sides = scatter_sides(attn_chunks, attn_corner)
    grad_q_half, grad_k_half, grad_v_half = after(
        (grad_q_half, grad_k_half, grad_v_half), attn_chunks
    )
    part_q = mm_nt(grad_q_half, w_q).reshape(2, local_len, width)
    part_kv = (mm_nt(grad_k_half, w_k) + mm_nt(grad_v_half, w_v)).reshape(2, seq, width)
    part_own = jnp.concatenate([part_q[0] + part_kv[0, :local_len], part_kv[0, local_len:]], axis=0)
    part_sib = jnp.concatenate([part_q[1] + part_kv[1, :local_len], part_kv[1, local_len:]], axis=0)
    part_img = part_own + core_swap(part_sib)
    part_far = part_img[local_len:].astype(bf16)
    part_far = y_swap(jnp.concatenate([part_far[:, half_w:], part_far[:, :half_w]], axis=1))
    grad_norm_one = part_img[:local_len] + part_far.astype(f32)
    grad_in = grad_resid + norm_backward(
        grad_norm_one, norm_img[:local_len], scale_img[:local_len], gain_one
    )
    grad_input = to_natural(grad_in)[None]

    zeros = jnp.zeros((half_w,), f32)
    sum_q = jnp.sum(grad_q, axis=0)
    sum_v = jnp.sum(grad_v, axis=0)

    def spread(vector):
        return jnp.where(
            first_core,
            jnp.concatenate([vector, zeros]),
            jnp.concatenate([zeros, vector]),
        )

    cols = jnp.stack(
        [
            jnp.sum(part_img * norm_img, axis=0),
            jnp.sum(part_img, axis=0),
            jnp.sum(grad_resid, axis=0),
            jnp.sum(grad_norm_two * norm_two, axis=0),
            jnp.sum(grad_norm_two, axis=0),
            jnp.sum(grad_rows, axis=0),
        ],
        axis=0,
    )
    cols = to_natural(cols).reshape(1, -1)
    bias_sum = jnp.sum(grad_pre, axis=0, keepdims=True)
    sums = jnp.concatenate(
        [cols, spread(sum_q)[None], spread(sum_v)[None], bias_sum], axis=1
    )
    sums = sums + y_swap(sums)
    mask = 2
    while mask < dp_count:
        sums = sums + dp_swap(sums, mask)
        mask *= 2
    sums_far = core_swap(sums)
    cols = (sums + sums_far)[0, : 8 * width].reshape(8, width)
    bias_mine, bias_far = sums[:, 8 * width :], sums_far[:, 8 * width :]

    down_sum = scatter_done(down_line, part_img)
    up_sum = scatter_done(up_line, part_img)
    attn_line = scatter_line(attn_sides, depth, part_img)
    attn_sum = scatter_done(attn_line)

    part_out = mm_nt(after(act_half, *attn_chunks), w_down)
    block_rows = resid + part_out[:local_len] + core_swap(part_out[local_len:]) + bias_d
    block_out = to_natural(block_rows)[None]

    def trade(values):
        upper, lower = values[:owned], values[owned:]
        mine = jnp.where(first_core, upper, lower)
        other = core_swap(jnp.where(first_core, lower, upper))
        return mine, other

    def join(mine, other):
        return jnp.where(
            first_core,
            jnp.concatenate([mine, other], axis=1),
            jnp.concatenate([other, mine], axis=1),
        )

    down_mine, down_other = trade(down_sum)
    up_mine, up_other = trade(up_sum)
    attn_mine, attn_other = trade(attn_sum)
    device_at = dp_at * ctx_count + y_at
    vec_sum = lax.dynamic_slice_in_dim(cols.T, device_at * owned, owned, axis=0)
    grad_attn = jnp.concatenate(
        [
            join(
                attn_mine[:, i * half_w : (i + 1) * half_w],
                attn_other[:, i * half_w : (i + 1) * half_w],
            )
            for i in range(4)
        ]
        + [vec_sum[:, :2], vec_sum[:, 6:8], vec_sum[:, 2:3]],
        axis=1,
    )
    grad_feed = jnp.concatenate(
        [join(up_mine, up_other), join(down_mine, down_other), vec_sum[:, 3:6]], axis=1
    )
    grad_up = join(bias_mine, bias_far).reshape(hidden)

    new_attn, new_attn_first, new_attn_second = adamw_step(
        attn_params, attn_first, attn_second, grad_attn
    )
    new_feed, new_feed_first, new_feed_second = adamw_step(
        feed_params, feed_first, feed_second, grad_feed
    )
    new_up, new_up_first, new_up_second = adamw_step(
        up_bias, up_bias_first, up_bias_second, grad_up
    )
    return (
        block_out,
        grad_input,
        grad_attn,
        grad_feed,
        grad_up,
        new_attn,
        new_attn_first,
        new_attn_second,
        new_feed,
        new_feed_first,
        new_feed_second,
        new_up,
        new_up_first,
        new_up_second,
    )


def solution(mesh):
    tokens = P("dp", "ctx", None)
    params = P(("dp", "ctx"), None)

    return jax.shard_map(
        body,
        mesh=mesh,
        in_specs=(tokens, tokens, P("dp", "ctx")) + (params,) * 6 + (P(),) * 3,
        out_specs=(tokens, tokens, params, params, P()) + (params,) * 6 + (P(),) * 3,
        check_vma=False,
    )
```

```python
import math

import jax
import jax.numpy as jnp
from jax import lax
from jax.experimental import pallas as pl
from jax.experimental.pallas import tpu as pltpu
from jax.sharding import PartitionSpec as P


HD = 72
STEP = 4


eps_norm = 1e-06
lr_rate = 0.01
beta_one = 0.9
beta_two = 0.999
eps_adam = 1e-08
decay_rate = 0.05

bf16 = jnp.bfloat16
f32 = jnp.float32


def gelu_tanh(values):
    return jax.nn.gelu(values, approximate=True)


def norm_stats(values):
    mean_val = jnp.mean(values, axis=-1, keepdims=True)
    centred = values - mean_val
    var_val = jnp.mean(centred * centred, axis=-1, keepdims=True)
    inv_std = lax.rsqrt(var_val + eps_norm)
    return centred * inv_std, inv_std


def norm_backward(grad_out, normed, inv_std, gain):
    scaled = grad_out * gain
    return inv_std * (
        scaled
        - jnp.mean(scaled, axis=-1, keepdims=True)
        - normed * jnp.mean(scaled * normed, axis=-1, keepdims=True)
    )


def adamw_step(param, first, second, grad):
    first_new = beta_one * first + (1.0 - beta_one) * grad
    second_new = beta_two * second + (1.0 - beta_two) * grad * grad
    first_hat = first_new / (1.0 - beta_one**STEP)
    second_hat = second_new / (1.0 - beta_two**STEP)
    param_new = param - lr_rate * (
        first_hat / (jnp.sqrt(second_hat) + eps_adam) + decay_rate * param
    )
    return (param_new, first_new, second_new)


def mm(left, right):
    return jnp.dot(left, right, preferred_element_type=f32)


def mm_nt(left, right):
    return lax.dot_general(left, right, (((1,), (1,)), ((), ())), preferred_element_type=f32)


def mm_tn(left, right):
    return lax.dot_general(left, right, (((0,), (0,)), ((), ())), preferred_element_type=f32)


def dp_swap(value, mask):
    count = lax.axis_size("dp")
    return lax.ppermute(value, "dp", [(i, i ^ mask) for i in range(count)])


def core_swap(value):
    return dp_swap(value, 1)


def x_swap(value):
    return dp_swap(value, 2)


def z_swap(value, step):
    return dp_swap(value, 4 * step)


def y_swap(value):
    count = lax.axis_size("ctx")
    return lax.ppermute(value, "ctx", [(i, i ^ 1) for i in range(count)])


def after(value, *others):
    return lax.optimization_barrier((value, others))[0]


def gather_line(block, depth):
    return [block] + [z_swap(block, step) for step in range(1, depth)]


def gather_sides(line, *others):
    whole = after(jnp.concatenate(line, axis=0), *others)
    return whole, x_swap(whole), y_swap(whole)


def gather_corner(sides, *others):
    whole, over_x, over_y = sides
    half = whole.shape[0] // 2
    send_x, send_y = after((over_x[:half], over_y[half:]), *others)
    return [whole, over_x, over_y, y_swap(send_x), x_swap(send_y)]


def gather_all(pieces):
    return jnp.concatenate(pieces, axis=0)


def add_half(left, right):
    return (left.astype(f32) + right.astype(f32)).astype(bf16)


def scatter_corner(corner, cut):
    split = corner.shape[0] * cut // 2
    from_y = y_swap(corner[:split]) if cut > 0 else None
    from_x = x_swap(corner[split:]) if cut < 2 else None
    return from_y, from_x


def scatter_sides(chunks, corners, *others):
    near, side_x, side_y = chunks
    from_y, from_x = after(corners, *others)
    if from_y is not None:
        split = from_y.shape[0]
        side_x = jnp.concatenate([add_half(side_x[:split], from_y), side_x[split:]], axis=0)
    if from_x is not None:
        split = near.shape[0] - from_x.shape[0]
        side_y = jnp.concatenate([side_y[:split], add_half(side_y[split:], from_x)], axis=0)
    return near, x_swap(side_x), y_swap(side_y)


def scatter_line(sides, depth, *others):
    near, got_x, got_y = after(sides, *others)
    total = (near.astype(f32) + got_x.astype(f32) + got_y.astype(f32)).astype(bf16)
    rows = total.shape[0] // depth
    parts = [total[step * rows : (step + 1) * rows] for step in range(depth)]
    return parts[:1] + [z_swap(parts[step], step) for step in range(1, depth)]


def scatter_done(parts, *others):
    parts = after(parts, *others)
    out = parts[0].astype(f32)
    for part in parts[1:]:
        out = out + part.astype(f32)
    return out


def weight_chunks(left, right):
    size = left.shape[1] // 4
    return [mm_tn(left[:, i * size : (i + 1) * size], right).astype(bf16) for i in range(3)]


def weight_corner(left, right):
    size = left.shape[1] // 4
    return mm_tn(left[:, 3 * size :], right).astype(bf16)


def split_two(values):
    high = lax.reduce_precision(values, 8, 7)
    return jnp.concatenate([high.astype(bf16), (values - high).astype(bf16)], axis=0)


def attend_kernel(packed_ref, valid_ref, mixed_ref, log_ref):
    rows, width = mixed_ref.shape[1:]
    live = valid_ref[0] > 0
    for head in range(width // HD):
        at = head * HD
        query = packed_ref[0, :rows, at : at + HD]
        key = packed_ref[0, :, width + at : width + at + HD]
        value = packed_ref[0, :, 2 * width + at : 2 * width + at + HD]
        scores = mm_nt(key, query) * (1.0 / math.sqrt(HD))
        scores = jnp.where(live, scores, -1e30)
        top = jnp.max(scores, axis=0, keepdims=True)
        prob = jnp.exp(scores - top)
        total = jnp.sum(prob, axis=0, keepdims=True)
        log_ref[0, head : head + 1, :] = top + jnp.log(total)
        half = (prob * (1.0 / total)).astype(bf16)
        mixed_ref[0, :, at : at + HD] = mm_tn(half, value).astype(bf16)


def attend(packed, valid, rows, width):
    images, seq, wide = packed.shape
    heads = width // HD
    return pl.pallas_call(
        attend_kernel,
        grid=(images,),
        in_specs=[pl.BlockSpec((1, seq, wide), lambda i: (i, 0, 0)), pl.BlockSpec((1, seq, 1), lambda i: (i, 0, 0))],
        out_specs=[pl.BlockSpec((1, rows, width), lambda i: (i, 0, 0)), pl.BlockSpec((1, heads, rows), lambda i: (i, 0, 0))],
        out_shape=[jax.ShapeDtypeStruct((images, rows, width), bf16), jax.ShapeDtypeStruct((images, heads, rows), f32)],
        compiler_params=pltpu.CompilerParams(vmem_limit_bytes=56 << 20),
        cost_estimate=pl.CostEstimate(flops=4*images*rows*seq*width, bytes_accessed=packed.size*2, transcendentals=images*heads*rows*seq),
    )(packed, valid)


def back_kernel(packed_ref, valid_ref, mixed_ref, log_ref, grad_ref, out_ref, sum_ref):
    rows, width = mixed_ref.shape[1:]
    seq, wide = out_ref.shape[1:]
    scale = 1.0 / math.sqrt(HD)
    live = valid_ref[0] > 0
    out_ref[0, rows:, :width] = jnp.zeros((seq - rows, width), bf16)
    if wide > 3 * width:
        out_ref[0, :, 3 * width :] = jnp.zeros((seq, wide - 3 * width), bf16)
    sum_ref[0] = jnp.zeros(sum_ref.shape[1:], f32)
    for head in range(width // HD):
        at = head * HD
        query = packed_ref[0, :rows, at : at + HD]
        key = packed_ref[0, :, width + at : width + at + HD]
        value = packed_ref[0, :, 2 * width + at : 2 * width + at + HD]
        grad = grad_ref[0, :, at : at + HD]
        mixed = mixed_ref[0, :, at : at + HD]
        delta = jnp.sum((grad.astype(f32) * mixed.astype(f32)).T, axis=0, keepdims=True)
        scores = mm_nt(key, query) * scale
        scores = jnp.where(live, scores, -1e30)
        prob = jnp.exp(scores - log_ref[0, head : head + 1, :])
        grad_v = mm(prob.astype(bf16), grad)
        grad_s = (prob * (mm_nt(value, grad) - delta)).astype(bf16)
        grad_k = mm(grad_s, query) * scale
        grad_q = mm_tn(grad_s, key) * scale
        out_ref[0, :rows, at : at + HD] = grad_q.astype(bf16)
        out_ref[0, :, width + at : width + at + HD] = grad_k.astype(bf16)
        out_ref[0, :, 2 * width + at : 2 * width + at + HD] = grad_v.astype(bf16)
        sum_ref[0, :1, at : at + HD] = jnp.sum(grad_q, axis=0, keepdims=True)
        sum_ref[0, :1, 2 * width + at : 2 * width + at + HD] = jnp.sum(grad_v, axis=0, keepdims=True)


def attend_back(packed, valid, mixed, log_total, grad):
    images, seq, wide = packed.shape
    rows, width = mixed.shape[1:]
    heads = width // HD

    def whole(shape):
        return pl.BlockSpec((1,) + shape, lambda i: (i, 0, 0))

    return pl.pallas_call(
        back_kernel,
        grid=(images,),
        in_specs=[whole((seq, wide)), whole((seq, 1)), whole((rows, width)), whole((heads, rows)), whole((rows, width))],
        out_specs=[whole((seq, wide)), whole((8, wide))],
        out_shape=[jax.ShapeDtypeStruct((images, seq, wide), bf16), jax.ShapeDtypeStruct((images, 8, wide), f32)],
        compiler_params=pltpu.CompilerParams(vmem_limit_bytes=56 << 20),
        cost_estimate=pl.CostEstimate(flops=10*images*rows*seq*width, bytes_accessed=packed.size*4, transcendentals=images*heads*rows*seq),
    )(packed, valid, mixed, log_total, grad)


def body(
    tokens_in,
    cotangent,
    token_mask,
    attn_params,
    attn_first,
    attn_second,
    feed_params,
    feed_first,
    feed_second,
    up_bias,
    up_bias_first,
    up_bias_second,
):
    images, local_len, width = tokens_in.shape
    hidden = up_bias.shape[0]
    owned = attn_params.shape[0]
    dp_count = lax.axis_size("dp")
    ctx_count = lax.axis_size("ctx")
    assert images == 1 and ctx_count == 2 and dp_count % 4 == 0
    depth = dp_count // 4
    dp_at = lax.axis_index("dp")
    y_at = lax.axis_index("ctx")
    core = dp_at % 2
    x_at = (dp_at // 2) % 2
    z_at = dp_at // 4
    first_core = core == 0
    half_w = width // 2
    half_h = hidden // 2

    rows_own = tokens_in[0]
    mask_own = token_mask.astype(f32)
    mask_img = jnp.concatenate([mask_own, y_swap(mask_own)], axis=1)
    mask_all = jnp.concatenate([mask_img, core_swap(mask_img)], axis=0)
    valid = mask_all[:, :, None]

    attn_half = attn_params.astype(bf16)
    feed_half = feed_params.astype(bf16)

    fill = -3 * half_w % 128
    packed_w = 3 * half_w + fill

    def pick(at):
        parts = [
            attn_half[:, i * width + at * half_w : i * width + (at + 1) * half_w]
            for i in range(4)
        ]
        parts.insert(3, jnp.zeros((owned, fill), bf16))
        parts.append(attn_half[:, 4 * width :])
        parts.append(feed_half[:, 2 * hidden :])
        for i in range(2):
            parts.append(feed_half[:, i * hidden + at * half_h : i * hidden + (at + 1) * half_h])
        return jnp.concatenate(parts, axis=1)

    part_zero, part_one = pick(0), pick(1)
    keep = jnp.where(first_core, part_zero, part_one)
    give = jnp.where(first_core, part_one, part_zero)
    got = core_swap(give)
    shard = jnp.concatenate(
        [jnp.where(first_core, keep, got), jnp.where(first_core, got, keep)], axis=0
    )
    vecs = attn_params.shape[1] - 4 * width + feed_params.shape[1] - 2 * hidden
    cut = packed_w + half_w + vecs
    line_a = gather_line(shard[:, :cut], depth)
    sides_a = gather_sides(line_a)
    all_a = gather_corner(sides_a)
    w_attn = gather_all(all_a)
    line_c = gather_line(after(shard[:, cut : cut + half_h], *line_a), depth)
    sides_c = gather_sides(line_c, *sides_a[1:])
    line_d = gather_line(after(shard[:, cut + half_h :], *line_c), depth)
    rows_far = y_swap(after(rows_own, shard))

    block = 2 * owned
    spot = after(jnp.arange(width, dtype=jnp.int32), shard)
    place = spot // block
    y_of = y_at ^ (place // (2 * depth))
    x_of = x_at ^ ((place // depth) % 2)
    z_of = z_at ^ (place % depth)
    core_of = (spot % block) // owned
    natural = (((z_of * 2 + x_of) * 2 + core_of) * 2 + y_of) * owned + spot % owned
    row_ids = lax.broadcasted_iota(jnp.int32, (width, width), 0)
    order = (row_ids == natural[None, :]).astype(bf16)

    def to_local(values):
        both = mm(split_two(values), order)
        return both[: values.shape[0]] + both[values.shape[0] :]

    def to_natural(values):
        both = mm_nt(split_two(values), order)
        return both[: values.shape[0]] + both[values.shape[0] :]


    w_qkv = w_attn[:, :packed_w]
    w_o = w_attn[:, packed_w : packed_w + half_w]
    vec = w_attn[:, packed_w + half_w :]
    vec_nat = mm(order, vec[:, 2:4])
    vec_t = vec.astype(f32).T
    gain_one, shift_one, bias_o = vec_t[0], vec_t[1], vec_t[4]
    gain_two, shift_two, bias_d = vec_t[5], vec_t[6], vec_t[7]
    bias_qv = jnp.where(first_core, vec_nat[:half_w], vec_nat[half_w:]).T
    bias_up = lax.optimization_barrier(up_bias.astype(bf16)).astype(f32)
    bias_up = jnp.where(first_core, bias_up[:half_h], bias_up[half_h:])

    live = mask_own.reshape(local_len, 1)
    grad_rows = to_local(after(cotangent[0], sides_a[0]) * live)
    grad_half = grad_rows.astype(bf16)
    grad_both = jnp.concatenate([grad_half, core_swap(grad_half)], axis=0)

    rows_img = mm(after(jnp.concatenate([rows_own, rows_far], axis=0), sides_a[0]), order)
    rows_in = rows_img[:local_len]
    norm_img, scale_img = norm_stats(rows_img)
    half_img = (norm_img * gain_one + shift_one).astype(bf16)
    half_far = core_swap(half_img)
    one_all = jnp.concatenate([half_img, half_far], axis=0)
    seq = 2 * local_len
    gap = jnp.zeros((half_w,), f32)
    bias_qkv = jnp.concatenate([bias_qv[0], gap, bias_qv[1], gap[:fill]])

    def project(left, right):
        return (mm(left, right) + bias_qkv).astype(bf16)

    packed = project(one_all, w_qkv).reshape(2, seq, packed_w)
    mixed, log_total = attend(packed, valid, local_len, half_w)
    all_c = gather_corner(sides_c, mixed)
    w_up = gather_all(all_c)
    sides_d = gather_sides(line_d, mixed, *sides_c[1:])
    mixed_rows = mixed.reshape(2 * local_len, half_w)
    part = mm_nt(mixed_rows, w_o)
    resid = rows_in + part[:local_len] + core_swap(part[local_len:]) + bias_o

    norm_two, scale_two = norm_stats(resid)
    half_two = (norm_two * gain_two + shift_two).astype(bf16)
    all_d = gather_corner(sides_d)
    w_down = gather_all(all_d)
    two_both = jnp.concatenate([half_two, core_swap(half_two)], axis=0)

    def activate(left, right):
        values = mm(left, right) + bias_up
        return values, gelu_tanh(values).astype(bf16)

    pre_act, act_half = activate(two_both, w_up)
    down_corner = scatter_corner(weight_corner(grad_both, act_half), 2)
    down_chunks = weight_chunks(grad_both, act_half)

    def activate_back(left, right):
        values = jax.vjp(gelu_tanh, pre_act)[1](mm(left, right))[0]
        return values, values.astype(bf16)

    grad_pre, grad_pre_half = activate_back(after(grad_both, *down_chunks), w_down)
    up_corner = scatter_corner(weight_corner(two_both, grad_pre_half), 0)
    part = mm_nt(grad_pre_half, w_up)
    part_far = core_swap(part[local_len:])
    up_chunks = weight_chunks(two_both, after(grad_pre_half, part))
    down_sides = scatter_sides(down_chunks, down_corner, part)
    grad_norm_two = part[:local_len] + after(part_far, up_chunks)
    grad_resid = grad_rows + norm_backward(grad_norm_two, norm_two, scale_two, gain_two)
    grad_resid_half = grad_resid.astype(bf16)
    resid_far = core_swap(grad_resid_half)
    up_sides = scatter_sides(up_chunks, up_corner, grad_resid_half)
    resid_both = jnp.concatenate([grad_resid_half, resid_far], axis=0)

    grad_mixed = mm(resid_both, w_o).astype(bf16).reshape(2, local_len, half_w)
    grad_packed, head_sums = attend_back(packed, valid, mixed, log_total, grad_mixed)
    grad_packed = grad_packed.reshape(2 * seq, packed_w)
    down_line = scatter_line(down_sides, depth, grad_packed)
    corner_all = jnp.concatenate(
        [weight_corner(one_all, grad_packed), weight_corner(resid_both, mixed_rows)],
        axis=1,
    )
    attn_corner = scatter_corner(corner_all, 1)
    up_line = scatter_line(up_sides, depth, corner_all)
    pieces = [weight_chunks(one_all, grad_packed), weight_chunks(resid_both, mixed_rows)]
    attn_chunks = [jnp.concatenate([piece[i] for piece in pieces], axis=1) for i in range(3)]
    attn_sides = scatter_sides(attn_chunks, attn_corner)
    grad_packed = after(grad_packed, attn_chunks)
    part = mm_nt(grad_packed, w_qkv)
    part_img = part[:seq] + core_swap(part[seq:])
    part_far = part_img[local_len:].astype(bf16)
    part_far = y_swap(jnp.concatenate([part_far[:, half_w:], part_far[:, :half_w]], axis=1))
    grad_norm_one = part_img[:local_len] + part_far.astype(f32)
    grad_in = grad_resid + norm_backward(
        grad_norm_one, norm_img[:local_len], scale_img[:local_len], gain_one
    )
    grad_input = to_natural(grad_in)[None]

    zeros = jnp.zeros((half_w,), f32)
    head_sum = jnp.sum(head_sums[:, 0], axis=0)
    sum_q = head_sum[:half_w]
    sum_v = head_sum[2 * half_w : 3 * half_w]

    def spread(vector):
        return jnp.where(
            first_core,
            jnp.concatenate([vector, zeros]),
            jnp.concatenate([zeros, vector]),
        )

    cols = jnp.stack(
        [
            jnp.sum(part_img * norm_img, axis=0),
            jnp.sum(part_img, axis=0),
            jnp.sum(grad_resid, axis=0),
            jnp.sum(grad_norm_two * norm_two, axis=0),
            jnp.sum(grad_norm_two, axis=0),
            jnp.sum(grad_rows, axis=0),
        ],
        axis=0,
    )
    cols = to_natural(cols).reshape(1, -1)
    bias_sum = jnp.sum(grad_pre, axis=0, keepdims=True)
    sums = jnp.concatenate(
        [cols, spread(sum_q)[None], spread(sum_v)[None], bias_sum], axis=1
    )
    sums = sums + y_swap(sums)
    mask = 2
    while mask < dp_count:
        sums = sums + dp_swap(sums, mask)
        mask *= 2
    sums_far = core_swap(sums)
    cols = (sums + sums_far)[0, : 8 * width].reshape(8, width)
    bias_mine, bias_far = sums[:, 8 * width :], sums_far[:, 8 * width :]

    down_sum = scatter_done(down_line, part_img)
    up_sum = scatter_done(up_line, part_img)
    attn_line = scatter_line(attn_sides, depth, part_img)
    attn_sum = scatter_done(attn_line)

    part_out = mm_nt(after(act_half, *attn_chunks), w_down)
    block_rows = resid + part_out[:local_len] + core_swap(part_out[local_len:]) + bias_d
    block_out = to_natural(block_rows)[None]

    def trade(values):
        upper, lower = values[:owned], values[owned:]
        mine = jnp.where(first_core, upper, lower)
        other = core_swap(jnp.where(first_core, lower, upper))
        return mine, other

    def join(mine, other):
        return jnp.where(
            first_core,
            jnp.concatenate([mine, other], axis=1),
            jnp.concatenate([other, mine], axis=1),
        )

    down_mine, down_other = trade(down_sum)
    up_mine, up_other = trade(up_sum)
    attn_mine, attn_other = trade(attn_sum)
    device_at = dp_at * ctx_count + y_at
    vec_sum = lax.dynamic_slice_in_dim(cols.T, device_at * owned, owned, axis=0)
    grad_attn = jnp.concatenate(
        [
            join(attn_mine[:, at : at + half_w], attn_other[:, at : at + half_w])
            for at in (0, half_w, 2 * half_w, packed_w)
        ]
        + [vec_sum[:, :2], vec_sum[:, 6:8], vec_sum[:, 2:3]],
        axis=1,
    )
    grad_feed = jnp.concatenate(
        [join(up_mine, up_other), join(down_mine, down_other), vec_sum[:, 3:6]], axis=1
    )
    grad_up = join(bias_mine, bias_far).reshape(hidden)

    new_attn, new_attn_first, new_attn_second = adamw_step(
        attn_params, attn_first, attn_second, grad_attn
    )
    new_feed, new_feed_first, new_feed_second = adamw_step(
        feed_params, feed_first, feed_second, grad_feed
    )
    new_up, new_up_first, new_up_second = adamw_step(
        up_bias, up_bias_first, up_bias_second, grad_up
    )
    return (
        block_out,
        grad_input,
        grad_attn,
        grad_feed,
        grad_up,
        new_attn,
        new_attn_first,
        new_attn_second,
        new_feed,
        new_feed_first,
        new_feed_second,
        new_up,
        new_up_first,
        new_up_second,
    )


def solution(mesh):
    tokens = P("dp", "ctx", None)
    params = P(("dp", "ctx"), None)

    return jax.shard_map(
        body,
        mesh=mesh,
        in_specs=(tokens, tokens, P("dp", "ctx")) + (params,) * 6 + (P(),) * 3,
        out_specs=(tokens, tokens, params, params, P()) + (params,) * 6 + (P(),) * 3,
        check_vma=False,
    )
```

```python
import math

import jax
import jax.numpy as jnp
from jax import lax
from jax.experimental import pallas as pl
from jax.experimental.pallas import tpu as pltpu
from jax.sharding import PartitionSpec as P


HD = 72
STEP = 4


eps_norm = 1e-06
lr_rate = 0.01
beta_one = 0.9
beta_two = 0.999
eps_adam = 1e-08
decay_rate = 0.05

bf16 = jnp.bfloat16
f32 = jnp.float32


def gelu_tanh(values):
    return jax.nn.gelu(values, approximate=True)


def norm_stats(values):
    mean_val = jnp.mean(values, axis=-1, keepdims=True)
    centred = values - mean_val
    var_val = jnp.mean(centred * centred, axis=-1, keepdims=True)
    inv_std = lax.rsqrt(var_val + eps_norm)
    return centred * inv_std, inv_std


def norm_backward(grad_out, normed, inv_std, gain):
    scaled = grad_out * gain
    return inv_std * (
        scaled
        - jnp.mean(scaled, axis=-1, keepdims=True)
        - normed * jnp.mean(scaled * normed, axis=-1, keepdims=True)
    )


def adamw_step(param, first, second, grad):
    first_new = beta_one * first + (1.0 - beta_one) * grad
    second_new = beta_two * second + (1.0 - beta_two) * grad * grad
    first_hat = first_new / (1.0 - beta_one**STEP)
    second_hat = second_new / (1.0 - beta_two**STEP)
    param_new = param - lr_rate * (
        first_hat / (jnp.sqrt(second_hat) + eps_adam) + decay_rate * param
    )
    return (param_new, first_new, second_new)


def mm(left, right):
    return jnp.dot(left, right, preferred_element_type=f32)


def mm_nt(left, right):
    return lax.dot_general(left, right, (((1,), (1,)), ((), ())), preferred_element_type=f32)


def mm_tn(left, right):
    return lax.dot_general(left, right, (((0,), (0,)), ((), ())), preferred_element_type=f32)


def dp_swap(value, mask):
    count = lax.axis_size("dp")
    return lax.ppermute(value, "dp", [(i, i ^ mask) for i in range(count)])


def core_swap(value):
    return dp_swap(value, 1)


def x_swap(value):
    return dp_swap(value, 2)


def z_swap(value, step):
    return dp_swap(value, 4 * step)


def y_swap(value):
    count = lax.axis_size("ctx")
    return lax.ppermute(value, "ctx", [(i, i ^ 1) for i in range(count)])


def after(value, *others):
    return lax.optimization_barrier((value, others))[0]


def gather_line(block, depth):
    return [block] + [z_swap(block, step) for step in range(1, depth)]


def gather_sides(line, *others):
    whole = after(jnp.concatenate(line, axis=0), *others)
    return whole, x_swap(whole), y_swap(whole)


def gather_corner(sides, *others):
    whole, over_x, over_y = sides
    half = whole.shape[0] // 2
    send_x, send_y = after((over_x[:half], over_y[half:]), *others)
    return [whole, over_x, over_y, y_swap(send_x), x_swap(send_y)]


def gather_all(pieces):
    return jnp.concatenate(pieces, axis=0)


def add_half(left, right):
    return (left.astype(f32) + right.astype(f32)).astype(bf16)


def scatter_corner(corner, cut):
    split = corner.shape[0] * cut // 2
    from_y = y_swap(corner[:split]) if cut > 0 else None
    from_x = x_swap(corner[split:]) if cut < 2 else None
    return from_y, from_x


def scatter_sides(chunks, corners, *others):
    near, side_x, side_y = chunks
    from_y, from_x = after(corners, *others)
    if from_y is not None:
        split = from_y.shape[0]
        side_x = jnp.concatenate([add_half(side_x[:split], from_y), side_x[split:]], axis=0)
    if from_x is not None:
        split = near.shape[0] - from_x.shape[0]
        side_y = jnp.concatenate([side_y[:split], add_half(side_y[split:], from_x)], axis=0)
    return near, x_swap(side_x), y_swap(side_y)


def scatter_line(sides, depth, *others):
    near, got_x, got_y = after(sides, *others)
    total = (near.astype(f32) + got_x.astype(f32) + got_y.astype(f32)).astype(bf16)
    rows = total.shape[0] // depth
    parts = [total[step * rows : (step + 1) * rows] for step in range(depth)]
    return parts[:1] + [z_swap(parts[step], step) for step in range(1, depth)]


def scatter_done(parts, *others):
    parts = after(parts, *others)
    out = parts[0].astype(f32)
    for part in parts[1:]:
        out = out + part.astype(f32)
    return out


def weight_chunks(left, right):
    size = left.shape[1] // 4
    return [mm_tn(left[:, i * size : (i + 1) * size], right).astype(bf16) for i in range(3)]


def weight_corner(left, right):
    size = left.shape[1] // 4
    return mm_tn(left[:, 3 * size :], right).astype(bf16)


def split_two(values):
    high = lax.reduce_precision(values, 8, 7)
    return jnp.concatenate([high.astype(bf16), (values - high).astype(bf16)], axis=0)


def attend_kernel(packed_ref, valid_ref, mixed_ref, log_ref):
    rows, width = mixed_ref.shape[1:]
    live = valid_ref[0] > 0
    for head in range(width // HD):
        at = head * HD
        query = packed_ref[0, :rows, at : at + HD]
        key = packed_ref[0, :, width + at : width + at + HD]
        value = packed_ref[0, :, 2 * width + at : 2 * width + at + HD]
        scores = mm_nt(key, query) * (1.0 / math.sqrt(HD))
        scores = jnp.where(live, scores, -1e30)
        top = jnp.max(scores, axis=0, keepdims=True)
        prob = jnp.exp(scores - top)
        total = jnp.sum(prob, axis=0, keepdims=True)
        log_ref[0, head : head + 1, :] = top + jnp.log(total)
        half = (prob * (1.0 / total)).astype(bf16)
        mixed_ref[0, :, at : at + HD] = mm_tn(half, value).astype(bf16)


def attend(packed, valid, rows, width):
    images, seq, wide = packed.shape
    heads = width // HD
    return pl.pallas_call(
        attend_kernel,
        grid=(images,),
        in_specs=[pl.BlockSpec((1, seq, wide), lambda i: (i, 0, 0)), pl.BlockSpec((1, seq, 1), lambda i: (i, 0, 0))],
        out_specs=[pl.BlockSpec((1, rows, width), lambda i: (i, 0, 0)), pl.BlockSpec((1, heads, rows), lambda i: (i, 0, 0))],
        out_shape=[jax.ShapeDtypeStruct((images, rows, width), bf16), jax.ShapeDtypeStruct((images, heads, rows), f32)],
        compiler_params=pltpu.CompilerParams(vmem_limit_bytes=56 << 20),
        cost_estimate=pl.CostEstimate(flops=4*images*rows*seq*width, bytes_accessed=packed.size*2, transcendentals=images*heads*rows*seq),
    )(packed, valid)


def back_kernel(packed_ref, valid_ref, mixed_ref, log_ref, grad_ref, out_ref, sum_ref):
    rows, width = mixed_ref.shape[1:]
    seq, wide = out_ref.shape[1:]
    scale = 1.0 / math.sqrt(HD)
    live = valid_ref[0] > 0
    out_ref[0, rows:, :width] = jnp.zeros((seq - rows, width), bf16)
    if wide > 3 * width:
        out_ref[0, :, 3 * width :] = jnp.zeros((seq, wide - 3 * width), bf16)
    sum_ref[0] = jnp.zeros(sum_ref.shape[1:], f32)
    for head in range(width // HD):
        at = head * HD
        query = packed_ref[0, :rows, at : at + HD]
        key = packed_ref[0, :, width + at : width + at + HD]
        value = packed_ref[0, :, 2 * width + at : 2 * width + at + HD]
        grad = grad_ref[0, :, at : at + HD]
        mixed = mixed_ref[0, :, at : at + HD]
        delta = jnp.sum((grad.astype(f32) * mixed.astype(f32)).T, axis=0, keepdims=True)
        scores = mm_nt(key, query) * scale
        scores = jnp.where(live, scores, -1e30)
        prob = jnp.exp(scores - log_ref[0, head : head + 1, :])
        grad_v = mm(prob.astype(bf16), grad)
        grad_s = (prob * (mm_nt(value, grad) - delta)).astype(bf16)
        grad_k = mm(grad_s, query) * scale
        grad_q = mm_tn(grad_s, key) * scale
        out_ref[0, :rows, at : at + HD] = grad_q.astype(bf16)
        out_ref[0, :, width + at : width + at + HD] = grad_k.astype(bf16)
        out_ref[0, :, 2 * width + at : 2 * width + at + HD] = grad_v.astype(bf16)
        sum_ref[0, :1, at : at + HD] = jnp.sum(grad_q, axis=0, keepdims=True)
        sum_ref[0, :1, 2 * width + at : 2 * width + at + HD] = jnp.sum(grad_v, axis=0, keepdims=True)


def attend_back(packed, valid, mixed, log_total, grad):
    images, seq, wide = packed.shape
    rows, width = mixed.shape[1:]
    heads = width // HD

    def whole(shape):
        return pl.BlockSpec((1,) + shape, lambda i: (i, 0, 0))

    return pl.pallas_call(
        back_kernel,
        grid=(images,),
        in_specs=[whole((seq, wide)), whole((seq, 1)), whole((rows, width)), whole((heads, rows)), whole((rows, width))],
        out_specs=[whole((seq, wide)), whole((8, wide))],
        out_shape=[jax.ShapeDtypeStruct((images, seq, wide), bf16), jax.ShapeDtypeStruct((images, 8, wide), f32)],
        compiler_params=pltpu.CompilerParams(vmem_limit_bytes=56 << 20),
        cost_estimate=pl.CostEstimate(flops=10*images*rows*seq*width, bytes_accessed=packed.size*4, transcendentals=images*heads*rows*seq),
    )(packed, valid, mixed, log_total, grad)


def body(
    tokens_in,
    cotangent,
    token_mask,
    attn_params,
    attn_first,
    attn_second,
    feed_params,
    feed_first,
    feed_second,
    up_bias,
    up_bias_first,
    up_bias_second,
):
    images, local_len, width = tokens_in.shape
    hidden = up_bias.shape[0]
    owned = attn_params.shape[0]
    dp_count = lax.axis_size("dp")
    ctx_count = lax.axis_size("ctx")
    assert images == 1 and ctx_count == 2 and dp_count % 4 == 0
    depth = dp_count // 4
    dp_at = lax.axis_index("dp")
    y_at = lax.axis_index("ctx")
    core = dp_at % 2
    x_at = (dp_at // 2) % 2
    z_at = dp_at // 4
    first_core = core == 0
    half_w = width // 2
    half_h = hidden // 2

    rows_own = tokens_in[0]
    mask_own = token_mask.astype(f32)
    mask_img = jnp.concatenate([mask_own, y_swap(mask_own)], axis=1)
    mask_all = jnp.concatenate([mask_img, core_swap(mask_img)], axis=0)
    valid = mask_all[:, :, None]

    attn_half = attn_params.astype(bf16)
    feed_half = feed_params.astype(bf16)

    fill = -3 * half_w % 128
    packed_w = 3 * half_w + fill

    def pick(at):
        parts = [
            attn_half[:, i * width + at * half_w : i * width + (at + 1) * half_w]
            for i in range(4)
        ]
        parts.insert(3, jnp.zeros((owned, fill), bf16))
        parts.append(attn_half[:, 4 * width :])
        parts.append(feed_half[:, 2 * hidden :])
        for i in range(2):
            parts.append(feed_half[:, i * hidden + at * half_h : i * hidden + (at + 1) * half_h])
        return jnp.concatenate(parts, axis=1)

    part_zero, part_one = pick(0), pick(1)
    keep = jnp.where(first_core, part_zero, part_one)
    give = jnp.where(first_core, part_one, part_zero)
    got = core_swap(give)
    shard = jnp.concatenate(
        [jnp.where(first_core, keep, got), jnp.where(first_core, got, keep)], axis=0
    )
    vecs = attn_params.shape[1] - 4 * width + feed_params.shape[1] - 2 * hidden
    cut = packed_w + half_w + vecs
    line_a = gather_line(shard[:, :cut], depth)
    rows_far = y_swap(after(rows_own, shard))
    sides_a = gather_sides(line_a, rows_far)
    all_a = gather_corner(sides_a)
    w_attn = gather_all(all_a)
    line_c = gather_line(after(shard[:, cut : cut + half_h], *line_a), depth)
    sides_c = gather_sides(line_c, *sides_a[1:])
    line_d = gather_line(after(shard[:, cut + half_h :], *line_c), depth)

    block = 2 * owned
    spot = after(jnp.arange(width, dtype=jnp.int32), shard)
    place = spot // block
    y_of = y_at ^ (place // (2 * depth))
    x_of = x_at ^ ((place // depth) % 2)
    z_of = z_at ^ (place % depth)
    core_of = (spot % block) // owned
    natural = (((z_of * 2 + x_of) * 2 + core_of) * 2 + y_of) * owned + spot % owned
    row_ids = lax.broadcasted_iota(jnp.int32, (width, width), 0)
    order = (row_ids == natural[None, :]).astype(bf16)

    def to_local(values):
        both = mm(split_two(values), order)
        return both[: values.shape[0]] + both[values.shape[0] :]

    def to_natural(values):
        both = mm_nt(split_two(values), order)
        return both[: values.shape[0]] + both[values.shape[0] :]


    w_qkv = w_attn[:, :packed_w]
    w_o = w_attn[:, packed_w : packed_w + half_w]
    vec = w_attn[:, packed_w + half_w :]
    vec_nat = mm(order, vec[:, 2:4])
    vec_t = vec.astype(f32).T
    gain_one, shift_one, bias_o = vec_t[0], vec_t[1], vec_t[4]
    gain_two, shift_two, bias_d = vec_t[5], vec_t[6], vec_t[7]
    bias_qv = jnp.where(first_core, vec_nat[:half_w], vec_nat[half_w:]).T
    bias_up = lax.optimization_barrier(up_bias.astype(bf16)).astype(f32)
    bias_up = jnp.where(first_core, bias_up[:half_h], bias_up[half_h:])

    live = mask_own.reshape(local_len, 1)
    grad_rows = to_local(after(cotangent[0], sides_a[0]) * live)
    grad_half = grad_rows.astype(bf16)
    grad_both = jnp.concatenate([grad_half, core_swap(grad_half)], axis=0)

    rows_img = mm(after(jnp.concatenate([rows_own, rows_far], axis=0), sides_a[0]), order)
    rows_in = rows_img[:local_len]

    def norm_one(values):
        normed, inv_std = norm_stats(values)
        return normed, inv_std, (normed * gain_one + shift_one).astype(bf16)

    norm_img, scale_img, half_img = norm_one(rows_img)
    half_far = core_swap(half_img)
    one_all = jnp.concatenate([half_img, half_far], axis=0)
    seq = 2 * local_len
    gap = jnp.zeros((half_w,), f32)
    bias_qkv = jnp.concatenate([bias_qv[0], gap, bias_qv[1], gap[:fill]])

    def project(left, right):
        return (mm(left, right) + bias_qkv).astype(bf16)

    packed = project(one_all, w_qkv).reshape(2, seq, packed_w)
    mixed, log_total = attend(packed, valid, local_len, half_w)
    all_c = gather_corner(sides_c, mixed)
    w_up = gather_all(all_c)
    sides_d = gather_sides(line_d, mixed, *sides_c[1:])
    mixed_rows = mixed.reshape(2 * local_len, half_w)
    part = mm_nt(mixed_rows, w_o)
    resid = rows_in + part[:local_len] + core_swap(part[local_len:]) + bias_o

    norm_two, scale_two = norm_stats(resid)
    half_two = (norm_two * gain_two + shift_two).astype(bf16)
    all_d = gather_corner(sides_d)
    w_down = gather_all(all_d)
    two_both = jnp.concatenate([half_two, core_swap(half_two)], axis=0)

    def activate(left, right):
        values = mm(left, right) + bias_up
        return values, gelu_tanh(values).astype(bf16)

    pre_act, act_half = activate(two_both, w_up)
    down_last = weight_corner(grad_both, act_half)
    down_chunks = weight_chunks(grad_both, act_half)
    down_last, down_chunks = after((down_last, down_chunks), *sides_d[1:])
    down_corner = scatter_corner(down_last, 2)

    def activate_back(left, right):
        values = jax.vjp(gelu_tanh, pre_act)[1](mm(left, right))[0]
        return values, values.astype(bf16)

    grad_pre, grad_pre_half = activate_back(after(grad_both, *down_chunks), w_down)
    up_corner = scatter_corner(weight_corner(two_both, grad_pre_half), 0)
    part = mm_nt(grad_pre_half, w_up)
    part_far = core_swap(part[local_len:])
    up_chunks = weight_chunks(two_both, after(grad_pre_half, part))
    down_sides = scatter_sides(down_chunks, down_corner, part)
    grad_norm_two = part[:local_len] + after(part_far, up_chunks)
    grad_resid = grad_rows + norm_backward(grad_norm_two, norm_two, scale_two, gain_two)
    grad_resid_half = grad_resid.astype(bf16)
    resid_far = core_swap(grad_resid_half)
    up_sides = scatter_sides(up_chunks, up_corner, grad_resid_half)
    resid_both = jnp.concatenate([grad_resid_half, resid_far], axis=0)

    def butterfly(values):
        values = values + y_swap(values)
        mask = 2
        while mask < dp_count:
            values = values + dp_swap(values, mask)
            mask = 2 * mask
        return values, core_swap(values)

    early = jnp.concatenate(
        [
            jnp.sum(grad_resid, axis=0, keepdims=True),
            jnp.sum(grad_norm_two * norm_two, axis=0, keepdims=True),
            jnp.sum(grad_norm_two, axis=0, keepdims=True),
            jnp.sum(grad_rows, axis=0, keepdims=True),
        ],
        axis=0,
    )
    early = jnp.concatenate(
        [to_natural(early).reshape(1, -1), jnp.sum(grad_pre, axis=0, keepdims=True)], axis=1
    )
    early_sum, early_far = butterfly(early)
    early_cols = (early_sum + early_far)[:, : 4 * width].reshape(4, width)
    bias_mine, bias_far = early_sum[:, 4 * width :], early_far[:, 4 * width :]

    grad_mixed = mm(resid_both, w_o).astype(bf16).reshape(2, local_len, half_w)
    grad_packed, head_sums = attend_back(packed, valid, mixed, log_total, grad_mixed)
    grad_packed = grad_packed.reshape(2 * seq, packed_w)
    down_line = scatter_line(down_sides, depth, grad_packed)
    corner_all = jnp.concatenate(
        [weight_corner(one_all, grad_packed), weight_corner(resid_both, mixed_rows)],
        axis=1,
    )
    attn_corner = scatter_corner(corner_all, 1)
    up_line = scatter_line(up_sides, depth, corner_all)
    pieces = [weight_chunks(one_all, grad_packed), weight_chunks(resid_both, mixed_rows)]
    attn_chunks = [jnp.concatenate([piece[i] for piece in pieces], axis=1) for i in range(3)]
    attn_sides = scatter_sides(attn_chunks, attn_corner)
    grad_packed = after(grad_packed, attn_chunks)
    part = mm_nt(grad_packed, w_qkv)
    part_img = part[:seq] + core_swap(part[seq:])
    part_far = part_img[local_len:].astype(bf16)
    part_far = y_swap(jnp.concatenate([part_far[:, half_w:], part_far[:, :half_w]], axis=1))
    grad_norm_one = part_img[:local_len] + part_far.astype(f32)
    grad_in = grad_resid + norm_backward(
        grad_norm_one, norm_img[:local_len], scale_img[:local_len], gain_one
    )
    grad_input = to_natural(grad_in)[None]

    zeros = jnp.zeros((half_w,), f32)
    head_sum = jnp.sum(head_sums[:, 0], axis=0)
    sum_q = head_sum[:half_w]
    sum_v = head_sum[2 * half_w : 3 * half_w]

    def spread(vector):
        return jnp.where(
            first_core,
            jnp.concatenate([vector, zeros]),
            jnp.concatenate([zeros, vector]),
        )

    late = jnp.concatenate(
        [
            jnp.sum(part_img * norm_img, axis=0, keepdims=True),
            jnp.sum(part_img, axis=0, keepdims=True),
        ],
        axis=0,
    )
    late = jnp.concatenate(
        [to_natural(late).reshape(1, -1), spread(sum_q)[None], spread(sum_v)[None]], axis=1
    )
    late_sum, late_far = butterfly(late)
    late_cols = (late_sum + late_far).reshape(4, width)

    down_sum = scatter_done(down_line, part_img)
    up_sum = scatter_done(up_line, part_img)
    attn_line = scatter_line(attn_sides, depth, late)
    attn_sum = scatter_done(attn_line)

    part_out = mm_nt(after(act_half, late), w_down)
    block_rows = resid + part_out[:local_len] + core_swap(part_out[local_len:]) + bias_d
    block_out = to_natural(block_rows)[None]

    def trade(values):
        upper, lower = values[:owned], values[owned:]
        mine = jnp.where(first_core, upper, lower)
        other = core_swap(jnp.where(first_core, lower, upper))
        return mine, other

    def join(mine, other):
        return jnp.where(
            first_core,
            jnp.concatenate([mine, other], axis=1),
            jnp.concatenate([other, mine], axis=1),
        )

    device_at = dp_at * ctx_count + y_at

    def own_rows(values):
        return lax.dynamic_slice_in_dim(values.T, device_at * owned, owned, axis=0)

    def finish_feed(down_sum, up_sum, early_cols):
        grad = jnp.concatenate(
            [join(*trade(up_sum)), join(*trade(down_sum)), own_rows(early_cols)[:, 1:]], axis=1
        )
        return (grad,) + adamw_step(feed_params, feed_first, feed_second, grad)

    grad_feed, new_feed, new_feed_first, new_feed_second = finish_feed(down_sum, up_sum, early_cols)
    attn_mine, attn_other = trade(attn_sum)
    grad_attn = jnp.concatenate(
        [
            join(attn_mine[:, at : at + half_w], attn_other[:, at : at + half_w])
            for at in (0, half_w, 2 * half_w, packed_w)
        ]
        + [own_rows(late_cols), own_rows(early_cols)[:, :1]],
        axis=1,
    )
    grad_up = join(bias_mine, bias_far).reshape(hidden)

    new_attn, new_attn_first, new_attn_second = adamw_step(
        attn_params, attn_first, attn_second, grad_attn
    )
    new_up, new_up_first, new_up_second = adamw_step(
        up_bias, up_bias_first, up_bias_second, grad_up
    )
    return (
        block_out,
        grad_input,
        grad_attn,
        grad_feed,
        grad_up,
        new_attn,
        new_attn_first,
        new_attn_second,
        new_feed,
        new_feed_first,
        new_feed_second,
        new_up,
        new_up_first,
        new_up_second,
    )


def solution(mesh):
    tokens = P("dp", "ctx", None)
    params = P(("dp", "ctx"), None)

    return jax.shard_map(
        body,
        mesh=mesh,
        in_specs=(tokens, tokens, P("dp", "ctx")) + (params,) * 6 + (P(),) * 3,
        out_specs=(tokens, tokens, params, params, P()) + (params,) * 6 + (P(),) * 3,
        check_vma=False,
    )
```

```python
import math

import jax
import jax.numpy as jnp
from jax import lax
from jax.experimental import pallas as pl
from jax.experimental.pallas import tpu as pltpu
from jax.sharding import PartitionSpec as P


HD = 72
STEP = 4


eps_norm = 1e-06
lr_rate = 0.01
beta_one = 0.9
beta_two = 0.999
eps_adam = 1e-08
decay_rate = 0.05

bf16 = jnp.bfloat16
f32 = jnp.float32


def gelu_pair(values):
    root = math.sqrt(2.0 / math.pi)
    square = values * values
    bent = jnp.tanh(root * (values + 0.044715 * (square * values)))
    value = 0.5 * values * (1.0 + bent)
    inner = root * (1.0 + (3.0 * 0.044715) * square)
    slope = 0.5 * (1.0 + bent) + 0.5 * values * ((1.0 - bent * bent) * inner)
    return value, slope


def norm_stats(values):
    mean_val = jnp.mean(values, axis=-1, keepdims=True)
    centred = values - mean_val
    var_val = jnp.mean(centred * centred, axis=-1, keepdims=True)
    inv_std = lax.rsqrt(var_val + eps_norm)
    return centred * inv_std, inv_std


def norm_backward(grad_out, normed, inv_std, gain):
    scaled = grad_out * gain
    return inv_std * (
        scaled
        - jnp.mean(scaled, axis=-1, keepdims=True)
        - normed * jnp.mean(scaled * normed, axis=-1, keepdims=True)
    )


def adamw_step(param, first, second, grad):
    first_new = beta_one * first + (1.0 - beta_one) * grad
    second_new = beta_two * second + (1.0 - beta_two) * grad * grad
    first_hat = first_new / (1.0 - beta_one**STEP)
    second_hat = second_new / (1.0 - beta_two**STEP)
    param_new = param - lr_rate * (
        first_hat / (jnp.sqrt(second_hat) + eps_adam) + decay_rate * param
    )
    return (param_new, first_new, second_new)


def mm(left, right):
    return jnp.dot(left, right, preferred_element_type=f32)


def mm_nt(left, right):
    return lax.dot_general(left, right, (((1,), (1,)), ((), ())), preferred_element_type=f32)


def mm_tn(left, right):
    return lax.dot_general(left, right, (((0,), (0,)), ((), ())), preferred_element_type=f32)


def dp_swap(value, mask):
    count = lax.axis_size("dp")
    return lax.ppermute(value, "dp", [(i, i ^ mask) for i in range(count)])


def core_swap(value):
    return dp_swap(value, 1)


def x_swap(value):
    return dp_swap(value, 2)


def z_swap(value, step):
    return dp_swap(value, 4 * step)


def y_swap(value):
    count = lax.axis_size("ctx")
    return lax.ppermute(value, "ctx", [(i, i ^ 1) for i in range(count)])


def after(value, *others):
    return lax.optimization_barrier((value, others))[0]


def gather_line(block, depth):
    return [block] + [z_swap(block, step) for step in range(1, depth)]


def gather_sides(line, *others):
    whole = after(jnp.concatenate(line, axis=0), *others)
    return whole, x_swap(whole), y_swap(whole)


def gather_corner(sides, *others):
    whole, over_x, over_y = sides
    half = whole.shape[0] // 2
    send_x, send_y = after((over_x[:half], over_y[half:]), *others)
    return [whole, over_x, over_y, y_swap(send_x), x_swap(send_y)]


def gather_all(pieces):
    return jnp.concatenate(pieces, axis=0)


def add_half(left, right):
    return (left.astype(f32) + right.astype(f32)).astype(bf16)


def scatter_corner(corner, cut):
    split = corner.shape[0] * cut // 2
    from_y = y_swap(corner[:split]) if cut > 0 else None
    from_x = x_swap(corner[split:]) if cut < 2 else None
    return from_y, from_x


def scatter_sides(chunks, corners, *others):
    near, side_x, side_y = chunks
    from_y, from_x = after(corners, *others)
    if from_y is not None:
        split = from_y.shape[0]
        side_x = jnp.concatenate([add_half(side_x[:split], from_y), side_x[split:]], axis=0)
    if from_x is not None:
        split = near.shape[0] - from_x.shape[0]
        side_y = jnp.concatenate([side_y[:split], add_half(side_y[split:], from_x)], axis=0)
    return near, x_swap(side_x), y_swap(side_y)


def scatter_line(sides, depth, *others):
    near, got_x, got_y = after(sides, *others)
    total = (near.astype(f32) + got_x.astype(f32) + got_y.astype(f32)).astype(bf16)
    rows = total.shape[0] // depth
    parts = [total[step * rows : (step + 1) * rows] for step in range(depth)]
    return parts[:1] + [z_swap(parts[step], step) for step in range(1, depth)]


def scatter_done(parts, *others):
    parts = after(parts, *others)
    out = parts[0].astype(f32)
    for part in parts[1:]:
        out = out + part.astype(f32)
    return out


def weight_chunks(left, right):
    size = left.shape[1] // 4
    return [mm_tn(left[:, i * size : (i + 1) * size], right).astype(bf16) for i in range(3)]


def weight_corner(left, right):
    size = left.shape[1] // 4
    return mm_tn(left[:, 3 * size :], right).astype(bf16)


def split_two(values):
    high = lax.reduce_precision(values, 8, 7)
    return jnp.concatenate([high.astype(bf16), (values - high).astype(bf16)], axis=0)


def attend_kernel(packed_ref, valid_ref, mixed_ref, log_ref):
    rows, width = mixed_ref.shape[1:]
    live = valid_ref[0] > 0
    for head in range(width // HD):
        at = head * HD
        query = packed_ref[0, :rows, at : at + HD]
        key = packed_ref[0, :, width + at : width + at + HD]
        value = packed_ref[0, :, 2 * width + at : 2 * width + at + HD]
        scores = mm_nt(key, query) * (1.0 / math.sqrt(HD))
        scores = jnp.where(live, scores, -1e30)
        top = jnp.max(scores, axis=0, keepdims=True)
        prob = jnp.exp(scores - top)
        total = jnp.sum(prob, axis=0, keepdims=True)
        log_ref[0, head : head + 1, :] = top + jnp.log(total)
        half = (prob * (1.0 / total)).astype(bf16)
        mixed_ref[0, :, at : at + HD] = mm_tn(half, value).astype(bf16)


def attend(packed, valid, rows, width):
    images, seq, wide = packed.shape
    heads = width // HD
    return pl.pallas_call(
        attend_kernel,
        grid=(images,),
        in_specs=[pl.BlockSpec((1, seq, wide), lambda i: (i, 0, 0)), pl.BlockSpec((1, seq, 1), lambda i: (i, 0, 0))],
        out_specs=[pl.BlockSpec((1, rows, width), lambda i: (i, 0, 0)), pl.BlockSpec((1, heads, rows), lambda i: (i, 0, 0))],
        out_shape=[jax.ShapeDtypeStruct((images, rows, width), bf16), jax.ShapeDtypeStruct((images, heads, rows), f32)],
        compiler_params=pltpu.CompilerParams(vmem_limit_bytes=56 << 20),
        cost_estimate=pl.CostEstimate(flops=4*images*rows*seq*width, bytes_accessed=packed.size*2, transcendentals=images*heads*rows*seq),
    )(packed, valid)


def back_kernel(packed_ref, valid_ref, mixed_ref, log_ref, grad_ref, out_ref, sum_ref):
    rows, width = mixed_ref.shape[1:]
    seq, wide = out_ref.shape[1:]
    scale = 1.0 / math.sqrt(HD)
    live = valid_ref[0] > 0
    out_ref[0, rows:, :width] = jnp.zeros((seq - rows, width), bf16)
    if wide > 3 * width:
        out_ref[0, :, 3 * width :] = jnp.zeros((seq, wide - 3 * width), bf16)
    sum_ref[0] = jnp.zeros(sum_ref.shape[1:], f32)
    for head in range(width // HD):
        at = head * HD
        query = packed_ref[0, :rows, at : at + HD]
        key = packed_ref[0, :, width + at : width + at + HD]
        value = packed_ref[0, :, 2 * width + at : 2 * width + at + HD]
        grad = grad_ref[0, :, at : at + HD]
        mixed = mixed_ref[0, :, at : at + HD]
        delta = jnp.sum((grad.astype(f32) * mixed.astype(f32)).T, axis=0, keepdims=True)
        scores = mm_nt(key, query) * scale
        scores = jnp.where(live, scores, -1e30)
        prob = jnp.exp(scores - log_ref[0, head : head + 1, :])
        grad_v = mm(prob.astype(bf16), grad)
        grad_s = (prob * (mm_nt(value, grad) - delta)).astype(bf16)
        grad_k = mm(grad_s, query) * scale
        grad_q = mm_tn(grad_s, key) * scale
        out_ref[0, :rows, at : at + HD] = grad_q.astype(bf16)
        out_ref[0, :, width + at : width + at + HD] = grad_k.astype(bf16)
        out_ref[0, :, 2 * width + at : 2 * width + at + HD] = grad_v.astype(bf16)
        sum_ref[0, :1, at : at + HD] = jnp.sum(grad_q, axis=0, keepdims=True)
        sum_ref[0, :1, 2 * width + at : 2 * width + at + HD] = jnp.sum(grad_v, axis=0, keepdims=True)


def attend_back(packed, valid, mixed, log_total, grad):
    images, seq, wide = packed.shape
    rows, width = mixed.shape[1:]
    heads = width // HD

    def whole(shape):
        return pl.BlockSpec((1,) + shape, lambda i: (i, 0, 0))

    return pl.pallas_call(
        back_kernel,
        grid=(images,),
        in_specs=[whole((seq, wide)), whole((seq, 1)), whole((rows, width)), whole((heads, rows)), whole((rows, width))],
        out_specs=[whole((seq, wide)), whole((8, wide))],
        out_shape=[jax.ShapeDtypeStruct((images, seq, wide), bf16), jax.ShapeDtypeStruct((images, 8, wide), f32)],
        compiler_params=pltpu.CompilerParams(vmem_limit_bytes=56 << 20),
        cost_estimate=pl.CostEstimate(flops=10*images*rows*seq*width, bytes_accessed=packed.size*4, transcendentals=images*heads*rows*seq),
    )(packed, valid, mixed, log_total, grad)


def body(
    tokens_in,
    cotangent,
    token_mask,
    attn_params,
    attn_first,
    attn_second,
    feed_params,
    feed_first,
    feed_second,
    up_bias,
    up_bias_first,
    up_bias_second,
):
    images, local_len, width = tokens_in.shape
    hidden = up_bias.shape[0]
    owned = attn_params.shape[0]
    dp_count = lax.axis_size("dp")
    ctx_count = lax.axis_size("ctx")
    assert images == 1 and ctx_count == 2 and dp_count % 4 == 0
    depth = dp_count // 4
    dp_at = lax.axis_index("dp")
    y_at = lax.axis_index("ctx")
    core = dp_at % 2
    x_at = (dp_at // 2) % 2
    z_at = dp_at // 4
    first_core = core == 0
    half_w = width // 2
    half_h = hidden // 2

    rows_own = tokens_in[0]
    mask_own = token_mask.astype(f32)
    mask_img = jnp.concatenate([mask_own, y_swap(mask_own)], axis=1)
    mask_all = jnp.concatenate([mask_img, core_swap(mask_img)], axis=0)
    valid = mask_all[:, :, None]

    attn_half = attn_params.astype(bf16)
    feed_half = feed_params.astype(bf16)

    vecs = attn_params.shape[1] - 4 * width + feed_params.shape[1] - 2 * hidden
    fill = -(3 * half_w + vecs) % 128 + vecs
    packed_w = 3 * half_w + fill

    def pick(at):
        halves = [
            attn_half[:, i * width + at * half_w : i * width + (at + 1) * half_w]
            for i in range(4)
        ]
        feeds = [
            feed_half[:, i * hidden + at * half_h : i * hidden + (at + 1) * half_h]
            for i in range(2)
        ]
        vectors = [attn_half[:, 4 * width :], feed_half[:, 2 * hidden :]]
        gap = [jnp.zeros((owned, fill - vecs), bf16)]
        return jnp.concatenate(
            halves[:3] + vectors + gap + [feeds[0], halves[3], feeds[1]], axis=1
        )

    part_zero, part_one = pick(0), pick(1)
    keep = jnp.where(first_core, part_zero, part_one)
    give = jnp.where(first_core, part_one, part_zero)
    got = core_swap(give)
    shard = jnp.concatenate(
        [jnp.where(first_core, keep, got), jnp.where(first_core, got, keep)], axis=0
    )
    cut_c = packed_w + half_h + half_w
    line_a = gather_line(shard[:, :packed_w], depth)
    rows_far = y_swap(after(rows_own, shard))
    sides_a = gather_sides(line_a, rows_far)
    all_a = gather_corner(sides_a)
    w_attn = gather_all(all_a)
    line_c = gather_line(after(shard[:, packed_w:cut_c], *line_a), depth)
    sides_c = gather_sides(line_c, *sides_a[1:])
    line_d = gather_line(after(shard[:, cut_c:], *line_c), depth)

    block = 2 * owned
    spot = after(jnp.arange(width, dtype=jnp.int32), shard)
    place = spot // block
    y_of = y_at ^ (place // (2 * depth))
    x_of = x_at ^ ((place // depth) % 2)
    z_of = z_at ^ (place % depth)
    core_of = (spot % block) // owned
    natural = (((z_of * 2 + x_of) * 2 + core_of) * 2 + y_of) * owned + spot % owned
    row_ids = lax.broadcasted_iota(jnp.int32, (width, width), 0)
    order = (row_ids == natural[None, :]).astype(bf16)

    def to_local(values):
        both = mm(split_two(values), order)
        return both[: values.shape[0]] + both[values.shape[0] :]

    def to_natural(values):
        both = mm_nt(split_two(values), order)
        return both[: values.shape[0]] + both[values.shape[0] :]


    w_qkv = w_attn
    vec = w_attn[:, 3 * half_w : 3 * half_w + vecs]
    vec_nat = mm(order, vec[:, 2:4])
    vec_t = vec.astype(f32).T
    gain_one, shift_one, bias_o = vec_t[0], vec_t[1], vec_t[4]
    gain_two, shift_two, bias_d = vec_t[5], vec_t[6], vec_t[7]
    bias_qv = jnp.where(first_core, vec_nat[:half_w], vec_nat[half_w:]).T
    bias_up = lax.optimization_barrier(up_bias.astype(bf16)).astype(f32)
    bias_up = jnp.where(first_core, bias_up[:half_h], bias_up[half_h:])

    live = mask_own.reshape(local_len, 1)
    grad_rows = to_local(after(cotangent[0], sides_a[0]) * live)
    grad_half = grad_rows.astype(bf16)
    grad_both = jnp.concatenate([grad_half, core_swap(grad_half)], axis=0)

    rows_img = mm(after(jnp.concatenate([rows_own, rows_far], axis=0), sides_a[0]), order)
    rows_in = rows_img[:local_len]

    def norm_one(values):
        normed, inv_std = norm_stats(values)
        return normed, inv_std, (normed * gain_one + shift_one).astype(bf16)

    norm_img, scale_img, half_img = norm_one(rows_img)
    half_far = core_swap(half_img)
    one_all = jnp.concatenate([half_img, half_far], axis=0)
    seq = 2 * local_len
    gap = jnp.zeros((half_w,), f32)
    bias_qkv = jnp.concatenate([bias_qv[0], gap, bias_qv[1], gap[:fill]])

    def project(left, right):
        return (mm(left, right) + bias_qkv).astype(bf16)

    packed = project(one_all, w_qkv).reshape(2, seq, packed_w)
    all_c = gather_corner(sides_c, packed)
    sides_d = gather_sides(line_d, packed, *sides_c[1:])
    mixed, log_total = attend(packed, valid, local_len, half_w)
    w_up = gather_all([piece[:, :half_h] for piece in all_c])
    w_o = gather_all([piece[:, half_h:] for piece in all_c])
    mixed_rows = mixed.reshape(2 * local_len, half_w)
    part = mm_nt(mixed_rows, w_o)
    resid = rows_in + part[:local_len] + core_swap(part[local_len:]) + bias_o

    norm_two, scale_two = norm_stats(resid)
    half_two = (norm_two * gain_two + shift_two).astype(bf16)
    all_d = gather_corner(sides_d)
    w_down = gather_all(all_d)
    two_both = jnp.concatenate([half_two, core_swap(half_two)], axis=0)

    def activate(left, right):
        values = mm(left, right) + bias_up
        value, slope = gelu_pair(values)
        return slope.astype(bf16), value.astype(bf16)

    slope_half, act_half = activate(two_both, w_up)
    down_last = weight_corner(grad_both, act_half)
    down_chunks = weight_chunks(grad_both, act_half)
    down_last, down_chunks = after((down_last, down_chunks), *sides_d[1:])
    down_corner = scatter_corner(down_last, 1)

    def activate_back(left, right):
        values = mm(left, right) * slope_half.astype(f32)
        return values, values.astype(bf16)

    grad_pre, grad_pre_half = activate_back(after(grad_both, *down_chunks), w_down)
    up_corner = scatter_corner(weight_corner(two_both, grad_pre_half), 1)
    part = mm_nt(grad_pre_half, w_up)
    part_far = core_swap(part[local_len:])
    up_chunks = weight_chunks(two_both, after(grad_pre_half, part))
    down_sides = scatter_sides(down_chunks, down_corner, part)
    grad_norm_two = part[:local_len] + after(part_far, up_chunks)
    grad_resid = grad_rows + norm_backward(grad_norm_two, norm_two, scale_two, gain_two)
    grad_resid_half = grad_resid.astype(bf16)
    resid_far = core_swap(grad_resid_half)
    up_sides = scatter_sides(up_chunks, up_corner, grad_resid_half)
    resid_both = jnp.concatenate([grad_resid_half, resid_far], axis=0)

    def butterfly(values):
        values = values + y_swap(values)
        mask = 2
        while mask < dp_count:
            values = values + dp_swap(values, mask)
            mask = 2 * mask
        return values, core_swap(values)

    early = jnp.concatenate(
        [
            jnp.sum(grad_resid, axis=0, keepdims=True),
            jnp.sum(grad_norm_two * norm_two, axis=0, keepdims=True),
            jnp.sum(grad_norm_two, axis=0, keepdims=True),
            jnp.sum(grad_rows, axis=0, keepdims=True),
        ],
        axis=0,
    )
    early = jnp.concatenate(
        [to_natural(early).reshape(1, -1), jnp.sum(grad_pre, axis=0, keepdims=True)], axis=1
    )
    early_sum, early_far = butterfly(early)
    early_cols = (early_sum + early_far)[:, : 4 * width].reshape(4, width)
    bias_mine, bias_far = early_sum[:, 4 * width :], early_far[:, 4 * width :]

    grad_mixed = mm(resid_both, w_o).astype(bf16).reshape(2, local_len, half_w)
    grad_packed, head_sums = attend_back(packed, valid, mixed, log_total, grad_mixed)
    grad_packed = grad_packed.reshape(2 * seq, packed_w)
    down_line = scatter_line(down_sides, depth, grad_packed)
    corner_all = jnp.concatenate(
        [weight_corner(one_all, grad_packed), weight_corner(resid_both, mixed_rows)],
        axis=1,
    )
    attn_corner = scatter_corner(corner_all, 1)
    up_line = scatter_line(up_sides, depth, corner_all)
    pieces = [weight_chunks(one_all, grad_packed), weight_chunks(resid_both, mixed_rows)]
    attn_chunks = [jnp.concatenate([piece[i] for piece in pieces], axis=1) for i in range(3)]
    attn_sides = scatter_sides(attn_chunks, attn_corner)
    grad_packed = after(grad_packed, attn_chunks)
    part = mm_nt(grad_packed, w_qkv)
    part_img = part[:seq] + core_swap(part[seq:])
    part_far = part_img[local_len:].astype(bf16)
    part_far = y_swap(jnp.concatenate([part_far[:, half_w:], part_far[:, :half_w]], axis=1))
    grad_norm_one = part_img[:local_len] + part_far.astype(f32)
    grad_in = grad_resid + norm_backward(
        grad_norm_one, norm_img[:local_len], scale_img[:local_len], gain_one
    )
    grad_input = to_natural(grad_in)[None]

    zeros = jnp.zeros((half_w,), f32)
    head_sum = jnp.sum(head_sums[:, 0], axis=0)
    sum_q = head_sum[:half_w]
    sum_v = head_sum[2 * half_w : 3 * half_w]

    def spread(vector):
        return jnp.where(
            first_core,
            jnp.concatenate([vector, zeros]),
            jnp.concatenate([zeros, vector]),
        )

    late = jnp.concatenate(
        [
            jnp.sum(part_img * norm_img, axis=0, keepdims=True),
            jnp.sum(part_img, axis=0, keepdims=True),
        ],
        axis=0,
    )
    late = jnp.concatenate(
        [to_natural(late).reshape(1, -1), spread(sum_q)[None], spread(sum_v)[None]], axis=1
    )
    late_sum, late_far = butterfly(late)
    late_cols = (late_sum + late_far).reshape(4, width)

    down_sum = scatter_done(down_line, part_img)
    up_sum = scatter_done(up_line, part_img)
    attn_line = scatter_line(attn_sides, depth, late)
    attn_sum = scatter_done(attn_line)

    part_out = mm_nt(after(act_half, late), w_down)
    block_rows = resid + part_out[:local_len] + core_swap(part_out[local_len:]) + bias_d
    block_out = to_natural(block_rows)[None]

    def trade(values):
        upper, lower = values[:owned], values[owned:]
        mine = jnp.where(first_core, upper, lower)
        other = core_swap(jnp.where(first_core, lower, upper))
        return mine, other

    def join(mine, other):
        return jnp.where(
            first_core,
            jnp.concatenate([mine, other], axis=1),
            jnp.concatenate([other, mine], axis=1),
        )

    device_at = dp_at * ctx_count + y_at

    def own_rows(values):
        return lax.dynamic_slice_in_dim(values.T, device_at * owned, owned, axis=0)

    def finish_feed(down_sum, up_sum, early_cols):
        grad = jnp.concatenate(
            [join(*trade(up_sum)), join(*trade(down_sum)), own_rows(early_cols)[:, 1:]], axis=1
        )
        return (grad,) + adamw_step(feed_params, feed_first, feed_second, grad)

    grad_feed, new_feed, new_feed_first, new_feed_second = finish_feed(down_sum, up_sum, early_cols)
    attn_mine, attn_other = trade(attn_sum)
    grad_attn = jnp.concatenate(
        [
            join(attn_mine[:, at : at + half_w], attn_other[:, at : at + half_w])
            for at in (0, half_w, 2 * half_w, packed_w)
        ]
        + [own_rows(late_cols), own_rows(early_cols)[:, :1]],
        axis=1,
    )
    grad_up = join(bias_mine, bias_far).reshape(hidden)

    new_attn, new_attn_first, new_attn_second = adamw_step(
        attn_params, attn_first, attn_second, grad_attn
    )
    new_up, new_up_first, new_up_second = adamw_step(
        up_bias, up_bias_first, up_bias_second, grad_up
    )
    return (
        block_out,
        grad_input,
        grad_attn,
        grad_feed,
        grad_up,
        new_attn,
        new_attn_first,
        new_attn_second,
        new_feed,
        new_feed_first,
        new_feed_second,
        new_up,
        new_up_first,
        new_up_second,
    )


def solution(mesh):
    tokens = P("dp", "ctx", None)
    params = P(("dp", "ctx"), None)

    return jax.shard_map(
        body,
        mesh=mesh,
        in_specs=(tokens, tokens, P("dp", "ctx")) + (params,) * 6 + (P(),) * 3,
        out_specs=(tokens, tokens, params, params, P()) + (params,) * 6 + (P(),) * 3,
        check_vma=False,
    )
```
